32 devices in a mesh: parts: 2 (over y), set: 4 (over x, core), seq: 4 (over z).
Axes of the slice: x: 2, y: 2, z: 4, core: 2. Of those that a mesh axis runs over, the one named last changes fastest.
Arguments:
- span_hidden: bfloat16 [512, 8192], P('parts', 'seq'), parts along dimension 0, may hold values from -500 to 500
- norm_gain: bfloat16 [8192], P('seq'), may hold values from 0.099609375 to 1.8984375
- key_value_weight: bfloat16 [8192, 2048], P('seq', 'set'), may hold values from -0.0625 to 0.0625
- prompt_key_value: bfloat16 [256, 2048], P(('parts', 'seq')), parts along dimension 0, may hold values from -6 to 6
- span_offset: int32 [2], P('parts'), parts along dimension 0, may hold values from 64 to 128
- cont_query: bfloat16 [32, 64, 8192], P(('parts', 'set', 'seq')), parts along dimension 0, may hold values from -24 to 24
- continuation_key_value: bfloat16 [32, 64, 2048], P(('parts', 'set', 'seq')), parts along dimension 0, may hold values from -6 to 6
- cont_lengths: int32 [32], P(('parts', 'set', 'seq')), parts along dimension 0, may hold values from 1 to 64
Outputs:
- span_key_value: bfloat16 [512, 2048], P(('parts', 'seq'), 'set'), parts along dimension 0
- attended: bfloat16 [32, 64, 8192], P(('parts', 'set', 'seq')), parts along dimension 0
The draws below stay inside these ranges and needn't reach their ends.
There are 2 independent parts, one for each index of `parts`. The reference program is written for one: setup_inputs(seed, part) draws one part's arguments, and reference() takes and returns one part's arrays. A program takes and returns all parts, laid end to end along the dimension named above; an argument that names none is the same for every part. Nothing has to cross between parts.
All inputs are finite; a program needn't handle non-finite values.
Results may differ from the reference program's by a relative error of at most 0.02.
Values may be sent and summed in bfloat16 or wider, within the bound.
A program may use at most 64 MiB of HBM per device.

```python
import math
import jax
import jax.numpy as jnp
from jax import lax

MODEL_WIDTH = 8192
QUERY_HEADS = 64
KEY_HEADS = 8
HEAD_SIZE = 128
SPAN_LENGTH = 256
CONTINUE_LENGTH = 64
PROMPT_LENGTH = 128
CONTINUATION_SET = 16


def draw_span_hidden(key, part):
    first, second = jax.random.split(jax.random.fold_in(key, 11), 2)
    columns = jnp.arange(MODEL_WIDTH).astype(jnp.float32) / MODEL_WIDTH
    ramp = 0.6 * 3.0 ** columns
    rough = jax.random.uniform(second, (MODEL_WIDTH,), jnp.float32, 0.5, 1.5)
    base = jnp.clip(jax.random.normal(first, (SPAN_LENGTH, MODEL_WIDTH), jnp.float32), -6.0, 6.0)
    result = base * (ramp * rough)[None, :]
    return result.astype(jnp.bfloat16)


def continuation_pair(key):
    query_key, kv_key = jax.random.split(jax.random.fold_in(key, 23), 2)
    key_value_shape = (CONTINUATION_SET, CONTINUE_LENGTH, 2 * KEY_HEADS * HEAD_SIZE)
    query_shape = (CONTINUATION_SET, CONTINUE_LENGTH, QUERY_HEADS * HEAD_SIZE)
    key_value_sample = jnp.clip(jax.random.normal(kv_key, key_value_shape, jnp.float32), -6.0, 6.0)
    query_draw = jnp.clip(jax.random.normal(query_key, query_shape, jnp.float32), -6.0, 6.0)
    return (query_draw, key_value_sample)


def draw_cont_query(key, part):
    return continuation_pair(key)[0].astype(jnp.bfloat16)


def draw_continuation_key_value(key, part):
    return continuation_pair(key)[1].astype(jnp.bfloat16)


def place_ends(drawn, stream_key, least, high):
    spot = [jax.random.randint(jax.random.fold_in(stream_key, axis), (), 0, length) for axis, length in enumerate(drawn.shape)]
    main_axis = drawn.shape.index(max(drawn.shape))
    next_to = spot[:main_axis] + [(spot[main_axis] + 1) % drawn.shape[main_axis]] + spot[main_axis + 1:]
    return drawn.at[tuple(spot)].set(least).at[tuple(next_to)].set(high)


def block_scale(stream_key, dims, cuts, least, largest):
    def one(position, blocks):
        draws = jax.random.uniform(jax.random.fold_in(jax.random.fold_in(stream_key, 6), position), (blocks,), jnp.float32, least / len(cuts), largest / len(cuts))
        return jnp.repeat(jnp.exp(draws), dims[position] // blocks).reshape((-1,) + (1,) * (len(dims) - position - 1))

    loudness = one(*cuts[0])
    for cut in cuts[1:]:
        loudness = loudness * one(*cut)
    return loudness


def bell_draw(stream_key, shape, spread, most, pieces=(), kind=jnp.bfloat16):
    loudness = block_scale(stream_key, shape, pieces, -0.22, 0.18) if pieces else 1.0
    entries = jax.random.normal(stream_key, shape, jnp.float32) * spread * loudness
    return jnp.minimum(jnp.maximum(entries, -most), most).astype(kind)


def setup_inputs(seed: int = 0, part: int = 0) -> dict:
    streams_of = jax.random.split(jax.random.key(seed), 9)
    own_keys = jax.random.split(jax.random.fold_in(streams_of[8], part), 9)
    span_hidden = draw_span_hidden(jax.random.fold_in(jax.random.fold_in(streams_of[8], part), 71), part)
    norm_gain = jnp.clip(1.0 + 0.18 * jax.random.normal(streams_of[1], (MODEL_WIDTH,), jnp.float32), 0.099609375, 1.8984375).astype(jnp.bfloat16)
    key_value_weight = bell_draw(streams_of[2], (MODEL_WIDTH, 2 * KEY_HEADS * HEAD_SIZE), MODEL_WIDTH ** -0.5, 0.0625, ((0, 4), (1, 4)))
    prompt_key_value = bell_draw(own_keys[3], (PROMPT_LENGTH, 2 * KEY_HEADS * HEAD_SIZE), 1.0, 6.0, ((0, 4),))
    span_offset = jax.random.randint(own_keys[4], (1,), PROMPT_LENGTH // 2, PROMPT_LENGTH + 1).astype(jnp.int32)
    cont_query = draw_cont_query(jax.random.fold_in(jax.random.fold_in(streams_of[8], part), 71), part)
    continuation_key_value = draw_continuation_key_value(jax.random.fold_in(jax.random.fold_in(streams_of[8], part), 71), part)
    cont_lengths = place_ends(jax.random.randint(own_keys[7], (CONTINUATION_SET,), 1, CONTINUE_LENGTH + 1), jax.random.fold_in(own_keys[7], 1), 1, CONTINUE_LENGTH).astype(jnp.int32)
    return dict(span_hidden=span_hidden, norm_gain=norm_gain, key_value_weight=key_value_weight, prompt_key_value=prompt_key_value, span_offset=span_offset, cont_query=cont_query, continuation_key_value=continuation_key_value, cont_lengths=cont_lengths)


EPS = 1e-05
NEGATIVE_LARGE = -1e+30

def frequencies(count, width, dtype):
    base = 500000.0 ** (-(jnp.arange(count).astype(dtype) * 2.0) / width)
    wave = 2.0 * math.pi / base
    smooth = (8192.0 / wave - 1.0) / 3.0
    blended = (1.0 - smooth) * base / 8.0 + smooth * base
    return jnp.where(wave < 2048.0, base, jnp.where(wave > 8192.0, base / 8.0, blended))

def apply_rotary(value_matrix, positions):
    mid_point = value_matrix.shape[-1] // 2
    frequency = frequencies(mid_point, value_matrix.shape[-1], value_matrix.dtype)
    angles = positions.astype(value_matrix.dtype)[:, None] * frequency[None, :]
    cosine = jnp.concatenate([jnp.cos(angles), jnp.cos(angles)], -1)[:, None, :]
    sine_part = jnp.concatenate([jnp.sin(angles), jnp.sin(angles)], -1)[:, None, :]
    turned = jnp.concatenate([-value_matrix[..., mid_point:], value_matrix[..., :mid_point]], -1)
    return value_matrix * cosine + turned * sine_part

def reference(span_hidden, norm_gain, key_value_weight, prompt_key_value, span_offset, cont_query, continuation_key_value, cont_lengths):
    key_columns_width = KEY_HEADS * HEAD_SIZE
    group_factor = QUERY_HEADS // KEY_HEADS
    hidden = span_hidden.astype(jnp.float32)
    mean_square = lax.optimization_barrier(jnp.sum(hidden * hidden, axis=1)) / MODEL_WIDTH
    normed = (hidden * lax.rsqrt(mean_square + EPS)[:, None] * norm_gain.astype(jnp.float32)[None, :]).astype(jnp.bfloat16)
    projected_rows = jnp.dot(normed, key_value_weight, preferred_element_type=jnp.float32)
    offset = span_offset[0]
    span_positions = offset + jnp.arange(SPAN_LENGTH, dtype=jnp.int32)
    rotary_applied = apply_rotary(projected_rows[:, :key_columns_width].reshape(SPAN_LENGTH, KEY_HEADS, HEAD_SIZE), span_positions).reshape(SPAN_LENGTH, key_columns_width)
    span_key_value = jnp.concatenate([rotary_applied, projected_rows[:, key_columns_width:]], 1).astype(jnp.bfloat16)
    prior_key_rows = jnp.concatenate([prompt_key_value[:, :key_columns_width], span_key_value[:, :key_columns_width]], 0).reshape(PROMPT_LENGTH + SPAN_LENGTH, KEY_HEADS, HEAD_SIZE)
    prior_value_rows = jnp.concatenate([prompt_key_value[:, key_columns_width:], span_key_value[:, key_columns_width:]], 0).reshape(PROMPT_LENGTH + SPAN_LENGTH, KEY_HEADS, HEAD_SIZE)
    past_valid = jnp.concatenate([jnp.arange(PROMPT_LENGTH, dtype=jnp.int32) < offset, jnp.ones((SPAN_LENGTH,), bool)])
    self_positions = offset + SPAN_LENGTH + jnp.arange(CONTINUE_LENGTH, dtype=jnp.int32)
    token_index = jnp.arange(CONTINUE_LENGTH, dtype=jnp.int32)
    causal = token_index[:, None] >= token_index[None, :]
    valid = jnp.concatenate([jnp.broadcast_to(past_valid[None, :], (CONTINUE_LENGTH, PROMPT_LENGTH + SPAN_LENGTH)), causal], 1)
    valid_four = valid[:, None, None, :]

    def score_one(item):
        query_raw, key_value_plain, sequence_length = item
        query_rows = apply_rotary(query_raw.astype(jnp.float32).reshape(CONTINUE_LENGTH, QUERY_HEADS, HEAD_SIZE), self_positions).astype(jnp.bfloat16)
        query_rows = query_rows.reshape(CONTINUE_LENGTH, KEY_HEADS, group_factor, HEAD_SIZE)
        self_key_rows = apply_rotary(key_value_plain[:, :key_columns_width].astype(jnp.float32).reshape(CONTINUE_LENGTH, KEY_HEADS, HEAD_SIZE), self_positions).astype(jnp.bfloat16)
        self_value_rows = key_value_plain[:, key_columns_width:].reshape(CONTINUE_LENGTH, KEY_HEADS, HEAD_SIZE)
        key_matrix = jnp.concatenate([prior_key_rows, self_key_rows], 0).astype(jnp.float32)
        vals = jnp.concatenate([prior_value_rows, self_value_rows], 0).astype(jnp.float32)
        scores = jnp.einsum('tgkd,ngd->tgkn', query_rows.astype(jnp.float32), key_matrix) * HEAD_SIZE ** (-0.5)
        masked = jnp.where(valid_four, scores, NEGATIVE_LARGE)
        top = lax.optimization_barrier(jnp.max(masked, axis=-1))
        weights = jnp.where(valid_four, jnp.exp(masked - top[..., None]), 0.0)
        total = lax.optimization_barrier(jnp.sum(weights, axis=-1))
        rounded = weights.astype(jnp.bfloat16).astype(jnp.float32)
        mixed = jnp.einsum('tgkn,ngd->tgkd', rounded, vals) / total[..., None]
        mixed = mixed.reshape(CONTINUE_LENGTH, QUERY_HEADS * HEAD_SIZE)
        live = token_index < sequence_length
        return jnp.where(live[:, None], mixed, 0.0).astype(jnp.bfloat16)
    attended = lax.map(score_one, (cont_query, continuation_key_value, cont_lengths))
    return (span_key_value, attended)
```

```python
import functools
import math

import jax
import jax.numpy as jnp
import numpy as np
from jax import lax
from jax.experimental import pallas as pl
from jax.experimental.pallas import tpu as pltpu
from jax.sharding import PartitionSpec as P

MODEL_WIDTH = 8192
QUERY_HEADS = 64
KEY_HEADS = 8
HEAD_SIZE = 128
GROUP = QUERY_HEADS // KEY_HEADS
KEY_COLUMNS = KEY_HEADS * HEAD_SIZE

EPS = 1e-05
NEGATIVE_LARGE = -1e30
EXPONENT = HEAD_SIZE ** (-0.5) * math.log2(math.e)

MESH = pl.DeviceIdType.MESH
HOP, PACE, TWIN_HOP = 2.9, 0.6, 1.0
F32 = jnp.float32
BF16 = jnp.bfloat16


def frequencies():
    index = np.arange(HEAD_SIZE // 2, dtype=np.float64)
    base = 500000.0 ** (-2.0 * index / HEAD_SIZE)
    wave = 2.0 * np.pi / base
    smooth = (8192.0 / wave - 1.0) / 3.0
    blended = (1.0 - smooth) * base / 8.0 + smooth * base
    table = np.where(wave < 2048.0, base, np.where(wave > 8192.0, base / 8.0, blended))
    return np.concatenate([table, table])


def rotary_constants(rows):
    frequency = frequencies()
    sign = np.where(np.arange(HEAD_SIZE) < HEAD_SIZE // 2, -1.0, 1.0)
    angles = np.arange(rows, dtype=np.float64)[:, None] * frequency
    ends = np.ones((8, HEAD_SIZE))
    cosine = np.concatenate([np.cos(angles), ends * frequency])
    sine = np.concatenate([sign * np.sin(angles), ends * sign])
    return np.stack([cosine, sine]).astype(np.float32)


def turn(value, cosine, sine):
    return value * cosine + pltpu.roll(value, HEAD_SIZE // 2, 1) * sine


def scores_of(query, keys):
    return lax.dot_general(query, keys, (((1,), (1,)), ((), ())), preferred_element_type=F32)


def with_ones(values):
    return jnp.concatenate([values, jnp.ones_like(values)], axis=1)


def kernel(
    n_set,
    n_seq,
    pieces,
    hidden_hbm,
    gain_hbm,
    weight_hbm,
    prompt_hbm,
    offset_smem,
    length_smem,
    query_hbm,
    own_hbm,
    rotary_hbm,
    span_out,
    attended_out,
    hidden,
    gain,
    weight,
    prompt,
    query_in,
    own,
    rotary,
    scaled,
    partial,
    sending,
    arriving,
    square_sum,
    square_theirs,
    turns,
    span,
    query,
    best,
    accum,
    load_sem,
    square_send,
    square_recv,
    sum_send,
    sum_recv,
    pz_send,
    pz_recv,
    px_send,
    px_recv,
    pc_send,
    pc_recv,
    sz_send,
    sz_recv,
    sx_send,
    sx_recv,
    sc_send,
    sc_recv,
):
    n_x = n_set // 2
    me_set = lax.axis_index("set")
    me_seq = lax.axis_index("seq")
    me_x, me_core = me_set // 2, me_set % 2
    length, features = hidden.shape
    width = weight.shape[1]
    rows = length // n_seq
    cached = prompt.shape[1] // n_seq
    tokens = query_in.shape[0]
    halves = 2 if width % 512 == 0 else 1
    half = width // halves
    per_set = width // HEAD_SIZE
    per_half = per_set // halves
    part = length // pieces
    chunks = [(j, r) for j in range(per_set) for r in range(pieces)]

    middle = n_seq // 2
    lower = me_seq < middle
    inward = jnp.where(lower, 1, -1)
    inner, outer = me_seq + inward, me_seq - inward
    is_end = jnp.logical_or(me_seq == 0, me_seq == n_seq - 1)
    not_end = jnp.logical_not(is_end)
    is_middle = jnp.logical_or(me_seq == middle - 1, me_seq == middle)
    not_middle = jnp.logical_not(is_middle)
    slot = jnp.where(is_middle, 1, 0)
    has_low, has_high = me_seq > 0, me_seq < n_seq - 1
    twin = me_x * 2 + 1 - me_core

    def set_at(step):
        return ((me_x + step) % n_x) * 2 + me_core

    def twin_at(step):
        return ((me_x + step) % n_x) * 2 + 1 - me_core

    def rows_of(which, count):
        return pl.ds(pl.multiple_of(which * count, count), count)

    loads = []

    def load(source, target):
        copy = pltpu.make_async_copy(source, target, load_sem.at[len(loads)])
        copy.start()
        loads.append(copy)
        return copy

    hidden_load = load(hidden_hbm, hidden)
    gain_load = load(gain_hbm, gain)
    prompt_loads = [
        load(
            prompt_hbm.at[:, pl.ds(s * width, width)],
            prompt.at[s, rows_of(me_seq, cached), :],
        )
        for s in range(n_set)
    ]
    weight_loads = [
        load(weight_hbm.at[:, pl.ds(i * half, half)], weight.at[:, pl.ds(i * half, half)])
        for i in range(halves)
    ]
    rotary_load = load(rotary_hbm, rotary)
    own_load = load(own_hbm.at[0], own)
    query_load = load(query_hbm.at[0], query_in)

    barrier = pltpu.get_barrier_semaphore()

    def greet(device):
        pl.semaphore_signal(barrier, inc=1, device_id=device, device_id_type=MESH)

    for e in range(1, n_x):
        greet({"set": set_at(e)})
    greet({"set": twin})

    @pl.when(has_low)
    def _():
        greet({"seq": me_seq - 1})

    @pl.when(has_high)
    def _():
        greet({"seq": me_seq + 1})

    waits = []

    def remote(source, target, send_sem, recv_sem, device):
        return pltpu.make_async_remote_copy(
            src_ref=source,
            dst_ref=target,
            send_sem=send_sem,
            recv_sem=recv_sem,
            device_id=device,
            device_id_type=MESH,
        )

    def book(*makes, when=None):
        waits.append((makes, when))
        return makes

    def start(makes):
        for make in makes:
            make().start()

    others = range(n_seq - 1)

    def other_seq(j):
        upper = (2 * me_seq) // n_seq
        low = j + (j - me_seq + n_seq) // n_seq
        down = n_seq - 1 - j
        high = down - (me_seq - down + n_seq) // n_seq
        return low + upper * (high - low)

    def prompt_block(s, z):
        return prompt.at[s, rows_of(z, cached), :]

    def span_block(s, c):
        j, r = chunks[c]
        return span.at[s * per_set + j, pl.ds(r * part, part), :]

    def chunk_of(ref, c):
        j, r = chunks[c]
        return ref.at[j, pl.ds(r * part, part), :]

    def project(i):
        columns = pl.ds(i * half, half)
        product = jnp.dot(scaled[...], weight[:, columns], preferred_element_type=F32)
        for j in range(per_half):
            partial[i * per_half + j] = product[:, j * HEAD_SIZE : (j + 1) * HEAD_SIZE]

    def sum_of(c):
        return lambda: remote(
            chunk_of(sending, c),
            chunk_of(arriving.at[slot], c),
            sum_send.at[c],
            sum_recv.at[slot, c],
            {"seq": inner},
        )

    def square_of():
        return remote(
            square_sum,
            square_theirs.at[slot],
            square_send.at[0],
            square_recv.at[slot],
            {"seq": inner},
        )

    sums = [sum_of(c) for c in range(len(chunks))]
    book(*sums)
    square_copies = book(square_of)

    def reduce_start(c):
        chunk_of(sending, c)[...] = chunk_of(partial, c)[...].astype(BF16)

    def reduce_more(c):
        come = chunk_of(arriving.at[0], c)
        remote(come, come, sum_send.at[c], sum_recv.at[0, c], {"seq": inner}).wait_recv()
        value = chunk_of(partial, c)[...] + come[...].astype(F32)
        chunk_of(partial, c)[...] = value
        chunk_of(sending, c)[...] = value.astype(BF16)

    def square_more():
        come = square_theirs.at[0]
        remote(come, come, square_send.at[0], square_recv.at[0], {"seq": inner}).wait_recv()
        square_sum[...] += come[...]

    def square_last():
        come = square_theirs.at[1]
        remote(come, come, square_send.at[0], square_recv.at[1], {"seq": inner}).wait_recv()
        total = square_sum[...] + come[...]
        column = jnp.broadcast_to(total[0:1, :], (HEAD_SIZE, length)).T
        inverse = lax.rsqrt(column / MODEL_WIDTH + EPS)
        is_key = me_set * width < KEY_COLUMNS
        cosine, sine = angles_at(0, length)
        turns[0] = jnp.where(is_key, cosine, 1.0) * inverse
        turns[1] = jnp.where(is_key, sine, 0.0) * inverse

    def angles_at(first, count):
        base = rotary.shape[1] - 8
        sign = rotary[1, base : base + 1, :]
        moved = rotary[0, base : base + 1, :] * offset_smem[0].astype(F32)
        cos_moved, sin_moved = jnp.cos(moved), jnp.sin(moved) * sign
        cosine, sine = rotary[0, first : first + count, :], rotary[1, first : first + count, :]
        return (
            cosine * cos_moved - sine * sin_moved,
            sine * cos_moved + cosine * sin_moved,
        )

    def finish(c):
        come = chunk_of(arriving.at[1], c)
        remote(come, come, sum_send.at[c], sum_recv.at[1, c], {"seq": inner}).wait_recv()
        block = chunk_of(partial, c)[...] + come[...].astype(F32)
        r = chunks[c][1]
        cosine, sine = (turns[k, pl.ds(r * part, part), :] for k in range(2))
        span_block(me_set, c)[...] = turn(block, cosine, sine).astype(BF16)

    def receive(c):
        mine = span_block(me_set, c)
        remote(mine, mine, sz_send.at[c], sz_recv.at[c], {"seq": outer}).wait_recv()

    def outward_of(c):
        mine = span_block(me_set, c)
        return lambda: remote(mine, mine, sz_send.at[c], sz_recv.at[c], {"seq": outer})

    def across_of(c, e):
        mine = span_block(me_set, c)
        return lambda: remote(
            mine, mine, sx_send.at[c, e], sx_recv.at[c, e], {"set": set_at(e)}
        )

    def twin_of(c, e):
        block = span_block(set_at(n_x - e), c)
        return lambda: remote(block, block, sc_send.at[c, e], sc_recv.at[c, e], {"set": twin})

    def count(make):
        return [make(c) for c in range(len(chunks))]

    outward = book(*count(outward_of), when=not_end)
    across = [book(*count(functools.partial(across_of, e=e))) for e in range(1, n_x)]
    twins = [book(*count(functools.partial(twin_of, e=e))) for e in range(n_x)]

    def spread(c):
        for copies in across:
            copies[c]().start()
        twins[0][c]().start()

    def cross(c):
        for e in range(1, n_x):
            come = span_block(set_at(n_x - e), c)
            remote(come, come, sx_send.at[c, e], sx_recv.at[c, e], {"set": twin}).wait_recv()
            twins[e][c]().start()

    def crossed(c):
        for e in range(n_x):
            come = span_block(twin_at(n_x - e), c)
            remote(come, come, sc_send.at[c, e], sc_recv.at[c, e], {"set": twin}).wait_recv()

    def prompt_side(device, side):
        block = prompt_block(me_set, me_seq)
        return lambda: remote(
            block, block, pz_send.at[me_seq, side], pz_recv.at[me_seq], {"seq": device}
        )

    prompt_low = book(prompt_side(me_seq - 1, 0), when=has_low)
    prompt_high = book(prompt_side(me_seq + 1, 1), when=has_high)

    def onward_of(j):
        z = other_seq(j)
        block = prompt_block(me_set, z)
        onward = me_seq + jnp.where(z < me_seq, 1, -1)
        there = jnp.logical_and(onward >= 0, onward < n_seq)
        make = lambda: remote(
            block, block, pz_send.at[z, 0], pz_recv.at[z], {"seq": onward}
        )
        book(make, when=there)
        return make, there

    def prompt_across_of(j, e):
        z = other_seq(j)
        block = prompt_block(me_set, z)
        return lambda: remote(
            block, block, px_send.at[z, e], px_recv.at[z, e], {"set": set_at(e)}
        )

    def prompt_twin_of(j, e):
        z = other_seq(j)
        block = prompt_block(set_at(n_x - e), z)
        return lambda: remote(
            block, block, pc_send.at[z, e], pc_recv.at[z, e], {"set": twin}
        )

    ahead = [onward_of(j) for j in others]
    prompt_across = [
        book(*[prompt_across_of(j, e) for j in others]) for e in range(1, n_x)
    ]
    prompt_twins = [book(*[prompt_twin_of(j, e) for j in others]) for e in range(n_x)]

    def pass_prompt(j, role):
        z = other_seq(j)
        block = prompt_block(me_set, z)
        remote(block, block, pz_send.at[z, 0], pz_recv.at[z], {"seq": z}).wait_recv()
        make, there = ahead[j]
        pl.when(there)(lambda: make().start())
        for copies in prompt_across:
            copies[j]().start()
        prompt_twins[0][j]().start()

    def cross_prompt(j, role):
        z = other_seq(j)
        for e in range(1, n_x):
            come = prompt_block(set_at(n_x - e), z)
            remote(come, come, px_send.at[z, e], px_recv.at[z, e], {"set": twin}).wait_recv()
            prompt_twins[e][j]().start()

    def crossed_prompt(j):
        z = other_seq(j)
        for e in range(n_x):
            come = prompt_block(twin_at(n_x - e), z)
            remote(come, come, pc_send.at[z, e], pc_recv.at[z, e], {"set": twin}).wait_recv()

    def columns_of(head):
        return pl.ds(head * HEAD_SIZE, HEAD_SIZE)

    causal = jnp.concatenate(
        [
            lax.broadcasted_iota(jnp.int32, (tokens, tokens), 0)
            >= lax.broadcasted_iota(jnp.int32, (tokens, tokens), 1)
        ]
        * GROUP,
        axis=0,
    )
    live = lax.broadcasted_iota(jnp.int32, (1, prompt.shape[1]), 1) < offset_smem[0]
    kept = lax.broadcasted_iota(jnp.int32, (tokens, HEAD_SIZE), 0) < length_smem[0]

    def turn_query(head, cosine, sine):
        for g in range(GROUP):
            raw = query_in[:, columns_of(head * GROUP + g)].astype(F32)
            query[head, g * tokens : (g + 1) * tokens, :] = turn(raw, cosine, sine).astype(BF16)

    def attend_own(head, cosine, sine):
        turn_query(head, cosine, sine)
        keys = turn(own[:, columns_of(head)].astype(F32), cosine, sine).astype(BF16)
        values = own[:, columns_of(head + KEY_HEADS)]
        scores = jnp.where(causal, scores_of(query[head], keys), NEGATIVE_LARGE)
        top = jnp.max(scores, axis=1, keepdims=True)
        weights = jnp.exp2((scores - top) * EXPONENT).astype(BF16)
        best[head] = jnp.broadcast_to(top, best.shape[1:])
        accum[head] = jnp.dot(weights, with_ones(values), preferred_element_type=F32)

    def prompt_head(head):
        return prompt[head // per_set, :, columns_of(head % per_set)]

    def attend_more(head, sources):
        parts = []
        for keys, values, mask in sources:
            scores = scores_of(query[head], keys)
            if mask is not None:
                scores = jnp.where(mask, scores, NEGATIVE_LARGE)
            parts.append((scores, values))
        old = best[head]
        top = old
        for scores, _ in parts:
            top = jnp.maximum(top, jnp.max(scores, axis=1, keepdims=True))
        total = accum[head] * jnp.concatenate([jnp.exp2((old - top) * EXPONENT)] * 2, axis=1)
        for scores, values in parts:
            spread_top = jnp.concatenate([top] * (scores.shape[1] // HEAD_SIZE), axis=1)
            weights = jnp.exp2((scores - spread_top) * EXPONENT).astype(BF16)
            total += jnp.dot(weights, with_ones(values), preferred_element_type=F32)
        return top, total

    def prompt_source(head):
        return prompt_head(head), prompt_head(head + KEY_HEADS), live

    def attend_prompt(head):
        top, total = attend_more(head, [prompt_source(head)])
        best[head] = top
        accum[head] = total

    def attend_last(head, with_prompt):
        sources = [(span[head], span[head + KEY_HEADS], None)]
        if with_prompt:
            sources = [prompt_source(head)] + sources
        _, total = attend_more(head, sources)
        mixed = total[:, :HEAD_SIZE] / total[:, HEAD_SIZE:]
        for g in range(GROUP):
            column = (head * GROUP + g) * HEAD_SIZE
            attended_out[:, column : column + HEAD_SIZE] = jnp.where(
                kept, mixed[g * tokens : (g + 1) * tokens, :], 0.0
            ).astype(BF16)

    hidden_load.wait()
    gain_load.wait()
    squares = jnp.zeros((length, HEAD_SIZE), F32)
    for i in range(features // HEAD_SIZE):
        block = hidden[:, i * HEAD_SIZE : (i + 1) * HEAD_SIZE]
        wide = block.astype(F32)
        squares += wide * wide
        scaled[:, i * HEAD_SIZE : (i + 1) * HEAD_SIZE] = block * gain[i : i + 1, :]
    turns[0] = squares
    for copy in prompt_loads:
        copy.wait()
    neighbours = n_x + jnp.where(has_low, 1, 0) + jnp.where(has_high, 1, 0)
    pl.semaphore_wait(barrier, neighbours)
    pl.when(has_low)(lambda: start(prompt_low))
    pl.when(has_high)(lambda: start(prompt_high))
    weight_loads[0].wait()
    project(0)

    hop, pace, twin_hop = HOP, PACE, TWIN_HOP
    n_chunks = len(chunks)
    agenda = []

    def at(time, do, who=None):
        agenda.append((time, len(agenda), who, do))

    def start_sum(c):
        reduce_start(c)
        sums[c]().start()

    def project_rest():
        for i in range(1, halves):
            weight_loads[i].wait()
            project(i)

    def sum_squares():
        square_row = jnp.sum(turns[0].T, axis=0, keepdims=True)
        square_sum[...] = jnp.broadcast_to(square_row, square_sum.shape)

    def more_sum(c):
        reduce_more(c)
        sums[c]().start()

    def more_square():
        square_more()
        start(square_copies)

    def finish_one(c):
        finish(c)
        pl.when(not_end)(lambda: outward[c]().start())
        spread(c)

    def receive_one(c):
        receive(c)
        pl.when(not_end)(lambda: outward[c]().start())
        spread(c)

    def ready_for_own():
        rotary_load.wait()
        own_load.wait()
        query_load.wait()

    def own_head(head):
        own_cosine, own_sine = angles_at(length, tokens)
        attend_own(head, own_cosine, own_sine)

    def store_span():
        for j in range(per_set):
            span_out[:, columns_of(j)] = span[me_set * per_set + j, rows_of(me_seq, rows), :]

    own_time, project_time = 0.33, 0.8
    at(0.1, sum_squares)
    at(0.15, lambda: start(square_copies), "end")
    at(0.2, project_rest)
    for c in range(n_chunks):
        when = 0.05 * c if c < per_half * pieces // 2 else project_time + pace * (c - 2)
        at(when, functools.partial(start_sum, c), "end")
    at(project_time, ready_for_own)
    for head in range(KEY_HEADS):
        at(project_time + own_time * (head + 0.5), functools.partial(own_head, head))
    for c in range(n_chunks):
        at(hop + pace * c, functools.partial(more_sum, c), "not_end")
        at(2 * hop + pace * c, functools.partial(finish_one, c), "middle")
        at(3 * hop + pace * c, functools.partial(cross, c), "middle")
        at(3 * hop + pace * c, functools.partial(receive_one, c), "not_middle")
        at(4 * hop + pace * c, functools.partial(cross, c), "not_middle")
    at(hop + 0.01, more_square, "not_end")
    at(2 * hop - 0.01, square_last, "middle")

    def prompt_at(j, role):
        if n_seq > 4:
            return 1 + 3 * j // (n_seq - 1)
        return max(1, j) if role == "middle" else j + 1

    for role in ("middle", "not_middle"):
        for j in others:
            far = prompt_at(j, role)
            at(far * hop - 0.05, functools.partial(pass_prompt, j, role), role)
            at((far + 1) * hop - 0.05, functools.partial(cross_prompt, j, role), role)
    prompt_there = 4 * hop + 0.7

    def all_prompt():
        for j in others:
            crossed_prompt(j)

    at(prompt_there, all_prompt)
    early = [h for h in range(KEY_HEADS) if h % per_set >= per_set // 2]
    for k, head in enumerate(early):
        at(prompt_there + 0.27 * k, functools.partial(attend_prompt, head))
    for j in range(per_set):
        arrived = 4 * hop + pace * ((j + 1) * pieces - 1) + twin_hop
        if j + 1 == per_set:
            at(arrived - 0.5, store_span)
        for r in range(pieces):
            at(arrived, functools.partial(crossed, j * pieces + r))
        for head in range(KEY_HEADS):
            if head % per_set == j:
                at(arrived, functools.partial(attend_last, head, head not in early))

    who_is = {
        "end": is_end,
        "not_end": not_end,
        "middle": is_middle,
        "not_middle": not_middle,
    }
    agenda.sort(key=lambda entry: entry[:2])
    while agenda:
        time, _, who, _ = agenda[0]
        group = []
        while agenda and agenda[0][2] == who and (who is not None or not group):
            group.append(agenda.pop(0)[3])

        def run(group=group):
            for do in group:
                do()

        if who is None:
            run()
        else:
            pl.when(who_is[who])(run)

    for makes, when in waits:

        def drain(makes=makes):
            for make in makes:
                make().wait_send()

        if when is None:
            drain()
        else:
            pl.when(when)(drain)


def hand_on(span_in, attended_in, span_out, attended_out, sem):
    copies = [
        pltpu.make_async_copy(attended_in, attended_out.at[0], sem.at[0]),
        pltpu.make_async_copy(span_in, span_out, sem.at[1]),
    ]
    for copy in copies:
        copy.start()
    for copy in copies:
        copy.wait()


def on_device(
    n_set,
    n_seq,
    span_hidden,
    norm_gain,
    key_value_weight,
    prompt_key_value,
    span_offset,
    cont_query,
    continuation_key_value,
    cont_lengths,
):
    length, features = span_hidden.shape
    width = key_value_weight.shape[1]
    rows = length // n_seq
    cached = prompt_key_value.shape[0]
    tokens = cont_query.shape[1]
    n_x = n_set // 2
    halves = 2 if width % 512 == 0 else 1
    pieces = 2
    per_set = width // HEAD_SIZE
    blocks = n_set * per_set
    chunks = per_set * pieces
    rotary = jnp.asarray(rotary_constants(length + tokens))
    gain = norm_gain.reshape(features // HEAD_SIZE, HEAD_SIZE)
    dma = pltpu.SemaphoreType.DMA
    anywhere = pl.BlockSpec(memory_space=pl.ANY)
    in_vmem = pl.BlockSpec(memory_space=pltpu.VMEM)
    in_smem = pl.BlockSpec(memory_space=pltpu.SMEM)

    def far(array):
        return pltpu.with_memory_space_constraint(array, pltpu.HBM)

    span_rows, attended = pl.pallas_call(
        functools.partial(kernel, n_set, n_seq, pieces),
        out_shape=(
            pltpu.VMEM((rows, width), BF16),
            pltpu.VMEM((tokens, QUERY_HEADS * HEAD_SIZE), BF16),
        ),
        in_specs=[
            anywhere,
            anywhere,
            anywhere,
            anywhere,
            in_smem,
            in_smem,
            anywhere,
            anywhere,
            anywhere,
        ],
        out_specs=(in_vmem, in_vmem),
        scratch_shapes=[
            pltpu.VMEM((length, features), BF16),
            pltpu.VMEM((features // HEAD_SIZE, HEAD_SIZE), BF16),
            pltpu.VMEM((features, width), BF16),
            pltpu.VMEM((n_set, cached * n_seq, width), BF16),
            pltpu.VMEM((tokens, QUERY_HEADS * HEAD_SIZE), BF16),
            pltpu.VMEM((tokens, 2 * KEY_COLUMNS), BF16),
            pltpu.VMEM(rotary.shape, F32),
            pltpu.VMEM((length, features), BF16),
            pltpu.VMEM((per_set, length, HEAD_SIZE), F32),
            pltpu.VMEM((per_set, length, HEAD_SIZE), BF16),
            pltpu.VMEM((2, per_set, length, HEAD_SIZE), BF16),
            pltpu.VMEM((8, length), F32),
            pltpu.VMEM((2, 8, length), F32),
            pltpu.VMEM((2, length, HEAD_SIZE), F32),
            pltpu.VMEM((blocks, length, HEAD_SIZE), BF16),
            pltpu.VMEM((KEY_HEADS, GROUP * tokens, HEAD_SIZE), BF16),
            pltpu.VMEM((KEY_HEADS, GROUP * tokens, HEAD_SIZE), F32),
            pltpu.VMEM((KEY_HEADS, GROUP * tokens, 2 * HEAD_SIZE), F32),
            dma((n_set + halves + 5,)),
            dma((1,)),
            dma((2,)),
            dma((chunks,)),
            dma((2, chunks)),
            dma((n_seq, 2)),
            dma((n_seq,)),
            dma((n_seq, n_x)),
            dma((n_seq, n_x)),
            dma((n_seq, n_x)),
            dma((n_seq, n_x)),
            dma((chunks,)),
            dma((chunks,)),
            dma((chunks, n_x)),
            dma((chunks, n_x)),
            dma((chunks, n_x)),
            dma((chunks, n_x)),
        ],
        compiler_params=pltpu.CompilerParams(
            collective_id=0, has_side_effects=True, vmem_limit_bytes=40 << 20
        ),
        name="project_gather_attend",
    )(
        far(span_hidden),
        far(gain),
        far(key_value_weight),
        far(prompt_key_value),
        span_offset,
        cont_lengths,
        far(cont_query),
        far(continuation_key_value),
        far(rotary),
    )
    return pl.pallas_call(
        hand_on,
        out_shape=(
            jax.ShapeDtypeStruct((rows, width), BF16),
            jax.ShapeDtypeStruct((1, tokens, QUERY_HEADS * HEAD_SIZE), BF16),
        ),
        in_specs=[in_vmem, in_vmem],
        out_specs=(anywhere, anywhere),
        scratch_shapes=[dma((2,))],
        compiler_params=pltpu.CompilerParams(vmem_limit_bytes=1 << 20),
        name="hand_on",
    )(span_rows, attended)


def solution(mesh):
    placed = (
        P("parts", "seq"),
        P("seq"),
        P("seq", "set"),
        P(("parts", "seq"), None),
        P("parts"),
        P(("parts", "set", "seq"), None, None),
        P(("parts", "set", "seq"), None, None),
        P(("parts", "set", "seq")),
    )
    return jax.shard_map(
        functools.partial(on_device, mesh.shape["set"], mesh.shape["seq"]),
        mesh=mesh,
        in_specs=placed,
        out_specs=(P(("parts", "seq"), "set"), P(("parts", "set", "seq"), None, None)),
        check_vma=False,
    )
```

```python
import functools
import math

import jax
import jax.numpy as jnp
import numpy as np
from jax import lax
from jax.experimental import pallas as pl
from jax.experimental.pallas import tpu as pltpu
from jax.sharding import PartitionSpec as P

MODEL_WIDTH = 8192
QUERY_HEADS = 64
KEY_HEADS = 8
HEAD_SIZE = 128
GROUP = QUERY_HEADS // KEY_HEADS
KEY_COLUMNS = KEY_HEADS * HEAD_SIZE

EPS = 1e-05
NEGATIVE_LARGE = -1e30
EXPONENT = HEAD_SIZE ** (-0.5) * math.log2(math.e)

MESH = pl.DeviceIdType.MESH
HOP, PACE, TWIN_HOP = 3.0, 0.65, 1.0
PASS = {"not_end": (2.85, 4.5, 6.8), "end": (5.0, 5.1, 7.5)}
CROSS = {"not_end": (8.0, 8.1, 10.4), "end": (8.05, 8.15, 10.5)}
SPLIT = 3
F32 = jnp.float32
BF16 = jnp.bfloat16


def frequencies():
    index = np.arange(HEAD_SIZE // 2, dtype=np.float64)
    base = 500000.0 ** (-2.0 * index / HEAD_SIZE)
    wave = 2.0 * np.pi / base
    smooth = (8192.0 / wave - 1.0) / 3.0
    blended = (1.0 - smooth) * base / 8.0 + smooth * base
    table = np.where(wave < 2048.0, base, np.where(wave > 8192.0, base / 8.0, blended))
    return np.concatenate([table, table])


def rotary_constants(rows):
    frequency = frequencies()
    sign = np.where(np.arange(HEAD_SIZE) < HEAD_SIZE // 2, -1.0, 1.0)
    angles = np.arange(rows, dtype=np.float64)[:, None] * frequency
    ends = np.ones((8, HEAD_SIZE))
    cosine = np.concatenate([np.cos(angles), ends * frequency])
    sine = np.concatenate([sign * np.sin(angles), ends * sign])
    return np.stack([cosine, sine]).astype(np.float32)


def turn(value, cosine, sine):
    return value * cosine + pltpu.roll(value, HEAD_SIZE // 2, 1) * sine


def scores_of(query, keys):
    return lax.dot_general(query, keys, (((1,), (1,)), ((), ())), preferred_element_type=F32)


def with_ones(values):
    return jnp.concatenate([values, jnp.ones_like(values)], axis=1)


def kernel(
    n_set,
    n_seq,
    pieces,
    hidden_hbm,
    gain_hbm,
    weight_hbm,
    prompt_hbm,
    offset_smem,
    length_smem,
    query_hbm,
    own_hbm,
    rotary_hbm,
    span_out,
    attended_out,
    hidden,
    gain,
    weight,
    prompt,
    query_in,
    own,
    rotary,
    scaled,
    partial,
    sending,
    arriving,
    square_sum,
    square_theirs,
    turns,
    span,
    query,
    best,
    accum,
    load_sem,
    square_send,
    square_recv,
    sum_send,
    sum_recv,
    pz_send,
    pz_recv,
    px_send,
    px_recv,
    pc_send,
    pc_recv,
    sz_send,
    sz_recv,
    sx_send,
    sx_recv,
    sc_send,
    sc_recv,
):
    n_x = n_set // 2
    me_set = lax.axis_index("set")
    me_seq = lax.axis_index("seq")
    me_x, me_core = me_set // 2, me_set % 2
    length, features = hidden.shape
    width = weight.shape[1]
    rows = length // n_seq
    cached = prompt.shape[1] // n_seq
    tokens = query_in.shape[0]
    halves = 2 if width % 512 == 0 else 1
    half = width // halves
    per_set = width // HEAD_SIZE
    per_half = per_set // halves
    part = length // pieces
    chunks = [(j, r) for j in range(per_set) for r in range(pieces)]

    middle = n_seq // 2
    lower = me_seq < middle
    inward = jnp.where(lower, 1, -1)
    inner, outer = me_seq + inward, me_seq - inward
    is_end = jnp.logical_or(me_seq == 0, me_seq == n_seq - 1)
    not_end = jnp.logical_not(is_end)
    is_middle = jnp.logical_or(me_seq == middle - 1, me_seq == middle)
    not_middle = jnp.logical_not(is_middle)
    slot = jnp.where(is_middle, 1, 0)
    has_low, has_high = me_seq > 0, me_seq < n_seq - 1
    twin = me_x * 2 + 1 - me_core

    def set_at(step):
        return ((me_x + step) % n_x) * 2 + me_core

    def twin_at(step):
        return ((me_x + step) % n_x) * 2 + 1 - me_core

    def rows_of(which, count):
        return pl.ds(pl.multiple_of(which * count, count), count)

    loads = []

    def load(source, target):
        copy = pltpu.make_async_copy(source, target, load_sem.at[len(loads)])
        copy.start()
        loads.append(copy)
        return copy

    hidden_load = load(hidden_hbm, hidden)
    gain_load = load(gain_hbm, gain)
    prompt_loads = [
        load(
            prompt_hbm.at[:, pl.ds(s * width, width)],
            prompt.at[s, rows_of(me_seq, cached), :],
        )
        for s in range(n_set)
    ]

    def load_weight(i):
        columns = pl.ds(i * half, half)
        return load(weight_hbm.at[:, columns], weight.at[:, columns])

    weight_loads = [load_weight(0)]

    barrier = pltpu.get_barrier_semaphore()

    def greet(device):
        pl.semaphore_signal(barrier, inc=1, device_id=device, device_id_type=MESH)

    others = range(n_seq - 1)

    def other_seq(j):
        upper = (2 * me_seq) // n_seq
        low = j + (j - me_seq + n_seq) // n_seq
        down = n_seq - 1 - j
        high = down - (me_seq - down + n_seq) // n_seq
        return low + upper * (high - low)

    def ends_at(z):
        return jnp.logical_or(z == 0, z == n_seq - 1)

    for e in range(1, n_x):
        greet({"set": set_at(e)})
    greet({"set": twin})
    for j in others:
        z = other_seq(j)
        sends_here = jnp.logical_or(jnp.logical_not(ends_at(z)), jnp.abs(z - me_seq) == 1)

        @pl.when(sends_here)
        def _(z=z):
            greet({"seq": z})

    waits = []

    def remote(source, target, send_sem, recv_sem, device):
        return pltpu.make_async_remote_copy(
            src_ref=source,
            dst_ref=target,
            send_sem=send_sem,
            recv_sem=recv_sem,
            device_id=device,
            device_id_type=MESH,
        )

    def book(make, when=None):
        waits.append((make, when))

    def start(makes):
        for make in makes:
            make().start()

    def prompt_block(s, z):
        return prompt.at[s, rows_of(z, cached), :]

    def span_block(s, c):
        j, r = chunks[c]
        return span.at[s * per_set + j, pl.ds(r * part, part), :]

    def chunk_of(ref, c):
        j, r = chunks[c]
        return ref.at[j, pl.ds(r * part, part), :]

    def project(i):
        columns = pl.ds(i * half, half)
        product = jnp.dot(scaled[...], weight[:, columns], preferred_element_type=F32)
        for j in range(per_half):
            partial[i * per_half + j] = product[:, j * HEAD_SIZE : (j + 1) * HEAD_SIZE]

    def sum_of(c):
        return lambda: remote(
            chunk_of(sending, c),
            chunk_of(arriving.at[slot], c),
            sum_send.at[0],
            sum_recv.at[slot, c],
            {"seq": inner},
        )

    def square_of():
        return remote(
            square_sum,
            square_theirs.at[slot],
            square_send.at[0],
            square_recv.at[slot],
            {"seq": inner},
        )

    sums = [sum_of(c) for c in range(len(chunks))]
    book(lambda: remote(sending, sending, sum_send.at[0], sum_recv.at[0, 0], {"seq": inner}))
    square_copies = [square_of]
    book(square_of)

    def reduce_start(c):
        chunk_of(sending, c)[...] = chunk_of(partial, c)[...].astype(BF16)

    def reduce_more(c):
        come = chunk_of(arriving.at[0], c)
        remote(come, come, sum_send.at[0], sum_recv.at[0, c], {"seq": inner}).wait_recv()
        value = chunk_of(partial, c)[...] + come[...].astype(F32)
        chunk_of(partial, c)[...] = value
        chunk_of(sending, c)[...] = value.astype(BF16)

    def square_more():
        come = square_theirs.at[0]
        remote(come, come, square_send.at[0], square_recv.at[0], {"seq": inner}).wait_recv()
        square_sum[...] += come[...]

    def square_last():
        come = square_theirs.at[1]
        remote(come, come, square_send.at[0], square_recv.at[1], {"seq": inner}).wait_recv()
        total = square_sum[...] + come[...]
        column = jnp.broadcast_to(total[0:1, :], (HEAD_SIZE, length)).T
        inverse = lax.rsqrt(column / MODEL_WIDTH + EPS)
        is_key = me_set * width < KEY_COLUMNS
        cosine, sine = angles_at(0, length)
        turns[0] = jnp.where(is_key, cosine, 1.0) * inverse
        turns[1] = jnp.where(is_key, sine, 0.0) * inverse

    def angles_at(first, count):
        base = rotary.shape[1] - 8
        sign = rotary[1, base : base + 1, :]
        moved = rotary[0, base : base + 1, :] * offset_smem[0].astype(F32)
        cos_moved, sin_moved = jnp.cos(moved), jnp.sin(moved) * sign
        cosine, sine = rotary[0, first : first + count, :], rotary[1, first : first + count, :]
        return (
            cosine * cos_moved - sine * sin_moved,
            sine * cos_moved + cosine * sin_moved,
        )

    def finish(c):
        come = chunk_of(arriving.at[1], c)
        remote(come, come, sum_send.at[0], sum_recv.at[1, c], {"seq": inner}).wait_recv()
        block = chunk_of(partial, c)[...] + come[...].astype(F32)
        r = chunks[c][1]
        cosine, sine = (turns[k, pl.ds(r * part, part), :] for k in range(2))
        span_block(me_set, c)[...] = turn(block, cosine, sine).astype(BF16)

    def receive(c):
        mine = span_block(me_set, c)
        remote(mine, mine, sz_send.at[0], sz_recv.at[c], {"seq": outer}).wait_recv()

    def outward_of(c):
        mine = span_block(me_set, c)
        return lambda: remote(mine, mine, sz_send.at[0], sz_recv.at[c], {"seq": outer})

    def across_of(c, e):
        mine = span_block(me_set, c)
        return lambda: remote(
            mine, mine, sx_send.at[e - 1], sx_recv.at[c, e - 1], {"set": set_at(e)}
        )

    def twin_of(c, e):
        block = span_block(set_at(n_x - e), c)
        return lambda: remote(block, block, sc_send.at[e], sc_recv.at[c, e], {"set": twin})

    def count(make):
        return [make(c) for c in range(len(chunks))]

    def span_set(s):
        return span.at[pl.ds(s * per_set, per_set)]

    outward = count(outward_of)
    across = [count(functools.partial(across_of, e=e)) for e in range(1, n_x)]
    twins = [count(functools.partial(twin_of, e=e)) for e in range(n_x)]
    whole = span_set(me_set)
    book(lambda: remote(whole, whole, sz_send.at[0], sz_recv.at[0], {"seq": outer}), not_end)
    for e in range(1, n_x):
        book(
            functools.partial(
                remote, whole, whole, sx_send.at[e - 1], sx_recv.at[0, e - 1], {"set": twin}
            )
        )
    for e in range(n_x):
        came = span_set(set_at(n_x - e))
        book(
            functools.partial(remote, came, came, sc_send.at[e], sc_recv.at[0, e], {"set": twin})
        )

    def spread(c):
        for copies in across:
            copies[c]().start()
        twins[0][c]().start()

    def cross(c):
        for e in range(1, n_x):
            come = span_block(set_at(n_x - e), c)
            remote(come, come, sx_send.at[e - 1], sx_recv.at[c, e - 1], {"set": twin}).wait_recv()
            twins[e][c]().start()

    def crossed(c):
        for e in range(n_x):
            come = span_block(twin_at(n_x - e), c)
            remote(come, come, sc_send.at[e], sc_recv.at[c, e], {"set": twin}).wait_recv()

    relays = jnp.logical_and(not_end, ends_at(outer))

    def prompt_to(source, z, which):
        block = prompt_block(me_set, source)
        return lambda: remote(
            block, block, pz_send.at[which, z], pz_recv.at[source], {"seq": z}
        )

    def prompt_across(z, e):
        block = prompt_block(me_set, z)
        return lambda: remote(
            block, block, px_send.at[z, e - 1], px_recv.at[z, e - 1], {"set": set_at(e)}
        )

    def prompt_twin(z, e):
        block = prompt_block(set_at(n_x - e), z)
        return lambda: remote(block, block, pc_send.at[z, e], pc_recv.at[z, e], {"set": twin})

    own_prompt, far_prompt = [], []
    for j in others:
        z = other_seq(j)
        reached = jnp.logical_or(not_end, z == inner)
        own_prompt.append((prompt_to(me_seq, z, 0), reached))
        passed = jnp.logical_and(relays, z != outer)
        far_prompt.append((prompt_to(outer, z, 1), passed))
        book(*own_prompt[-1])
        book(*far_prompt[-1])
        for e in range(1, n_x):
            book(prompt_across(z, e))
        for e in range(n_x):
            book(prompt_twin(z, e))

    def send_prompt():
        for make, when in reversed(own_prompt):
            pl.when(when)(lambda make=make: make().start())

    def pass_prompt(j):
        z = other_seq(j)
        block = prompt_block(me_set, z)
        remote(block, block, pz_send.at[0, z], pz_recv.at[z], {"seq": z}).wait_recv()

        @pl.when(jnp.logical_and(relays, z == outer))
        def _():
            for make, when in far_prompt:
                pl.when(when)(lambda make=make: make().start())

        for e in range(1, n_x):
            prompt_across(z, e)().start()
        prompt_twin(z, 0)().start()

    def cross_prompt(j):
        z = other_seq(j)
        for e in range(1, n_x):
            come = prompt_block(set_at(n_x - e), z)
            remote(
                come, come, px_send.at[z, e - 1], px_recv.at[z, e - 1], {"set": twin}
            ).wait_recv()
            prompt_twin(z, e)().start()

    def crossed_prompt(j):
        z = other_seq(j)
        for e in range(n_x):
            come = prompt_block(twin_at(n_x - e), z)
            remote(come, come, pc_send.at[z, e], pc_recv.at[z, e], {"set": twin}).wait_recv()

    def columns_of(head):
        return pl.ds(head * HEAD_SIZE, HEAD_SIZE)

    causal = jnp.concatenate(
        [
            lax.broadcasted_iota(jnp.int32, (tokens, tokens), 0)
            >= lax.broadcasted_iota(jnp.int32, (tokens, tokens), 1)
        ]
        * GROUP,
        axis=0,
    )
    live = lax.broadcasted_iota(jnp.int32, (1, prompt.shape[1]), 1) < offset_smem[0]
    kept = lax.broadcasted_iota(jnp.int32, (tokens, HEAD_SIZE), 0) < length_smem[0]

    def turn_query(head, cosine, sine):
        for g in range(GROUP):
            raw = query_in[:, columns_of(head * GROUP + g)].astype(F32)
            query[head, g * tokens : (g + 1) * tokens, :] = turn(raw, cosine, sine).astype(BF16)

    def attend_own(head, cosine, sine):
        turn_query(head, cosine, sine)
        keys = turn(own[:, columns_of(head)].astype(F32), cosine, sine).astype(BF16)
        values = own[:, columns_of(head + KEY_HEADS)]
        scores = jnp.where(causal, scores_of(query[head], keys), NEGATIVE_LARGE)
        top = jnp.max(scores, axis=1, keepdims=True)
        weights = jnp.exp2((scores - top) * EXPONENT).astype(BF16)
        best[head] = jnp.broadcast_to(top, best.shape[1:])
        accum[head] = jnp.dot(weights, with_ones(values), preferred_element_type=F32)

    def prompt_head(head):
        return prompt[head // per_set, :, columns_of(head % per_set)]

    def attend_more(head, sources):
        parts = []
        for keys, values, mask in sources:
            scores = scores_of(query[head], keys)
            if mask is not None:
                scores = jnp.where(mask, scores, NEGATIVE_LARGE)
            parts.append((scores, values))
        old = best[head]
        top = old
        for scores, _ in parts:
            top = jnp.maximum(top, jnp.max(scores, axis=1, keepdims=True))
        total = accum[head] * jnp.concatenate([jnp.exp2((old - top) * EXPONENT)] * 2, axis=1)
        for scores, values in parts:
            spread_top = jnp.concatenate([top] * (scores.shape[1] // HEAD_SIZE), axis=1)
            weights = jnp.exp2((scores - spread_top) * EXPONENT).astype(BF16)
            total += jnp.dot(weights, with_ones(values), preferred_element_type=F32)
        return top, total

    def prompt_source(head):
        return prompt_head(head), prompt_head(head + KEY_HEADS), live

    def attend_prompt(head):
        top, total = attend_more(head, [prompt_source(head)])
        best[head] = top
        accum[head] = total

    def attend_last(head, with_prompt):
        sources = [(span[head], span[head + KEY_HEADS], None)]
        if with_prompt:
            sources = [prompt_source(head)] + sources
        _, total = attend_more(head, sources)
        mixed = total[:, :HEAD_SIZE] / total[:, HEAD_SIZE:]
        for g in range(GROUP):
            column = (head * GROUP + g) * HEAD_SIZE
            attended_out[:, column : column + HEAD_SIZE] = jnp.where(
                kept, mixed[g * tokens : (g + 1) * tokens, :], 0.0
            ).astype(BF16)

    hidden_load.wait()
    gain_load.wait()
    squares = jnp.zeros((length, HEAD_SIZE), F32)
    for i in range(features // HEAD_SIZE):
        block = hidden[:, i * HEAD_SIZE : (i + 1) * HEAD_SIZE]
        wide = block.astype(F32)
        squares += wide * wide
        scaled[:, i * HEAD_SIZE : (i + 1) * HEAD_SIZE] = block * gain[i : i + 1, :]
    turns[0] = squares
    for copy in prompt_loads:
        copy.wait()
    weight_loads.extend(load_weight(i) for i in range(1, halves))
    rotary_load = load(rotary_hbm, rotary)
    own_load = load(own_hbm.at[0], own)
    query_load = load(query_hbm.at[0], query_in)
    def meet():
        lines = jnp.where(is_end, 1, n_seq - 1)
        pl.semaphore_wait(barrier, n_x + lines)
        send_prompt()

    pl.when(is_end)(meet)
    weight_loads[0].wait()
    project(0)

    hop, pace, twin_hop = HOP, PACE, TWIN_HOP
    n_chunks = len(chunks)
    agenda = []

    def at(time, do, who=None):
        agenda.append((time, len(agenda), who, do))

    def start_sum(c):
        reduce_start(c)
        sums[c]().start()

    def project_rest():
        for i in range(1, halves):
            weight_loads[i].wait()
            project(i)

    def sum_squares():
        square_row = jnp.sum(turns[0].T, axis=0, keepdims=True)
        square_sum[...] = jnp.broadcast_to(square_row, square_sum.shape)

    def more_sum(c):
        reduce_more(c)
        sums[c]().start()

    def more_square():
        square_more()
        start(square_copies)

    def finish_one(c):
        finish(c)
        pl.when(not_end)(lambda: outward[c]().start())
        spread(c)

    def receive_one(c):
        receive(c)
        pl.when(not_end)(lambda: outward[c]().start())
        spread(c)

    def ready_for_own():
        rotary_load.wait()
        own_load.wait()
        query_load.wait()

    def own_heads(heads):
        own_cosine, own_sine = angles_at(length, tokens)
        for head in heads:
            attend_own(head, own_cosine, own_sine)

    def store_span():
        for j in range(per_set):
            span_out[:, columns_of(j)] = span[me_set * per_set + j, rows_of(me_seq, rows), :]

    own_time, project_time = 0.33, 0.8
    at(project_time + 0.05, meet, "not_end")
    at(0.1, sum_squares)
    at(0.15, lambda: start(square_copies), "end")
    at(0.2, project_rest)
    for c in range(n_chunks):
        when = 0.05 * c if c < per_half * pieces // 2 else project_time + pace * (c - 2)
        at(when, functools.partial(start_sum, c), "end")
    at(project_time, ready_for_own)
    for head in range(0, KEY_HEADS, 2):
        heads = range(head, head + 2)
        at(project_time + own_time * (head + 0.5), functools.partial(own_heads, heads))
    for c in range(n_chunks):
        at(hop + pace * c, functools.partial(more_sum, c), "not_end")
        at(2 * hop + pace * c, functools.partial(finish_one, c), "middle")
        at(3 * hop + pace * c, functools.partial(cross, c), "middle")
        at(3 * hop + pace * c, functools.partial(receive_one, c), "not_middle")
        at(4 * hop + pace * c, functools.partial(cross, c), "not_middle")
    at(hop + 0.01, more_square, "not_end")
    at(2 * hop - 0.01, square_last, "middle")

    for j in others:
        step = min(2, j * 3 // (n_seq - 1))
        for who in ("not_end", "end"):
            at(PASS[who][step], functools.partial(pass_prompt, j), who)
            at(CROSS[who][step], functools.partial(cross_prompt, j), who)

    def all_prompt():
        for j in others:
            crossed_prompt(j)

    def prompt_heads(heads):
        for head in heads:
            attend_prompt(head)

    groups = [[h for h in range(KEY_HEADS) if h % per_set == j] for j in range(per_set)]
    split = min(SPLIT, per_set)
    for j in range(per_set):
        arrived = 4 * hop + pace * ((j + 1) * pieces - 1) + twin_hop
        if j + 1 == per_set:
            at(arrived - 0.5, store_span)

        def last_heads(j=j):
            if j == 0:
                all_prompt()
            for r in range(pieces):
                crossed(j * pieces + r)
            for head in groups[j]:
                attend_last(head, j < split)

        if j == split:
            for k in range(split, per_set):
                at(arrived - 0.6, functools.partial(prompt_heads, groups[k]))
        at(arrived, last_heads)

    who_is = {
        "end": is_end,
        "not_end": not_end,
        "middle": is_middle,
        "not_middle": not_middle,
    }
    agenda.sort(key=lambda entry: entry[:2])
    while agenda:
        time, _, who, _ = agenda[0]
        group = []
        while agenda and agenda[0][2] == who and (who is not None or not group):
            group.append(agenda.pop(0)[3])

        def run(group=group):
            for do in group:
                do()

        if who is None:
            run()
        else:
            pl.when(who_is[who])(run)

    for make, when in waits:
        if when is None:
            make().wait_send()
        else:
            pl.when(when)(lambda make=make: make().wait_send())


def hand_on(span_in, attended_in, span_out, attended_out, sem):
    copies = [
        pltpu.make_async_copy(attended_in, attended_out.at[0], sem.at[0]),
        pltpu.make_async_copy(span_in, span_out, sem.at[1]),
    ]
    for copy in copies:
        copy.start()
    for copy in copies:
        copy.wait()


def on_device(
    n_set,
    n_seq,
    span_hidden,
    norm_gain,
    key_value_weight,
    prompt_key_value,
    span_offset,
    cont_query,
    continuation_key_value,
    cont_lengths,
):
    length, features = span_hidden.shape
    width = key_value_weight.shape[1]
    rows = length // n_seq
    cached = prompt_key_value.shape[0]
    tokens = cont_query.shape[1]
    n_x = n_set // 2
    halves = 2 if width % 512 == 0 else 1
    pieces = 2
    per_set = width // HEAD_SIZE
    blocks = n_set * per_set
    chunks = per_set * pieces
    rotary = jnp.asarray(rotary_constants(length + tokens))
    gain = norm_gain.reshape(features // HEAD_SIZE, HEAD_SIZE)
    dma = pltpu.SemaphoreType.DMA
    anywhere = pl.BlockSpec(memory_space=pl.ANY)
    in_vmem = pl.BlockSpec(memory_space=pltpu.VMEM)
    in_smem = pl.BlockSpec(memory_space=pltpu.SMEM)

    def far(array):
        return pltpu.with_memory_space_constraint(array, pltpu.HBM)

    span_rows, attended = pl.pallas_call(
        functools.partial(kernel, n_set, n_seq, pieces),
        out_shape=(
            pltpu.VMEM((rows, width), BF16),
            pltpu.VMEM((tokens, QUERY_HEADS * HEAD_SIZE), BF16),
        ),
        in_specs=[
            anywhere,
            anywhere,
            anywhere,
            anywhere,
            in_smem,
            in_smem,
            anywhere,
            anywhere,
            anywhere,
        ],
        out_specs=(in_vmem, in_vmem),
        scratch_shapes=[
            pltpu.VMEM((length, features), BF16),
            pltpu.VMEM((features // HEAD_SIZE, HEAD_SIZE), BF16),
            pltpu.VMEM((features, width), BF16),
            pltpu.VMEM((n_set, cached * n_seq, width), BF16),
            pltpu.VMEM((tokens, QUERY_HEADS * HEAD_SIZE), BF16),
            pltpu.VMEM((tokens, 2 * KEY_COLUMNS), BF16),
            pltpu.VMEM(rotary.shape, F32),
            pltpu.VMEM((length, features), BF16),
            pltpu.VMEM((per_set, length, HEAD_SIZE), F32),
            pltpu.VMEM((per_set, length, HEAD_SIZE), BF16),
            pltpu.VMEM((2, per_set, length, HEAD_SIZE), BF16),
            pltpu.VMEM((8, length), F32),
            pltpu.VMEM((2, 8, length), F32),
            pltpu.VMEM((2, length, HEAD_SIZE), F32),
            pltpu.VMEM((blocks, length, HEAD_SIZE), BF16),
            pltpu.VMEM((KEY_HEADS, GROUP * tokens, HEAD_SIZE), BF16),
            pltpu.VMEM((KEY_HEADS, GROUP * tokens, HEAD_SIZE), F32),
            pltpu.VMEM((KEY_HEADS, GROUP * tokens, 2 * HEAD_SIZE), F32),
            dma((n_set + halves + 5,)),
            dma((1,)),
            dma((2,)),
            dma((1,)),
            dma((2, chunks)),
            dma((2, n_seq)),
            dma((n_seq,)),
            dma((n_seq, n_x - 1)),
            dma((n_seq, n_x - 1)),
            dma((n_seq, n_x)),
            dma((n_seq, n_x)),
            dma((1,)),
            dma((chunks,)),
            dma((n_x - 1,)),
            dma((chunks, n_x - 1)),
            dma((n_x,)),
            dma((chunks, n_x)),
        ],
        compiler_params=pltpu.CompilerParams(
            collective_id=0, has_side_effects=True, vmem_limit_bytes=40 << 20
        ),
        name="project_gather_attend",
    )(
        far(span_hidden),
        far(gain),
        far(key_value_weight),
        far(prompt_key_value),
        span_offset,
        cont_lengths,
        far(cont_query),
        far(continuation_key_value),
        far(rotary),
    )
    return pl.pallas_call(
        hand_on,
        out_shape=(
            jax.ShapeDtypeStruct((rows, width), BF16),
            jax.ShapeDtypeStruct((1, tokens, QUERY_HEADS * HEAD_SIZE), BF16),
        ),
        in_specs=[anywhere, anywhere],
        out_specs=(anywhere, anywhere),
        scratch_shapes=[dma((2,))],
        compiler_params=pltpu.CompilerParams(vmem_limit_bytes=1 << 20),
        name="hand_on",
    )(span_rows, attended)


def solution(mesh):
    placed = (
        P("parts", "seq"),
        P("seq"),
        P("seq", "set"),
        P(("parts", "seq"), None),
        P("parts"),
        P(("parts", "set", "seq"), None, None),
        P(("parts", "set", "seq"), None, None),
        P(("parts", "set", "seq")),
    )
    return jax.shard_map(
        functools.partial(on_device, mesh.shape["set"], mesh.shape["seq"]),
        mesh=mesh,
        in_specs=placed,
        out_specs=(P(("parts", "seq"), "set"), P(("parts", "set", "seq"), None, None)),
        check_vma=False,
    )
```

```python
import functools
import math

import jax
import jax.numpy as jnp
import numpy as np
from jax import lax
from jax.experimental import pallas as pl
from jax.experimental.pallas import tpu as pltpu
from jax.sharding import PartitionSpec as P

MODEL_WIDTH = 8192
QUERY_HEADS = 64
KEY_HEADS = 8
HEAD_SIZE = 128
GROUP = QUERY_HEADS // KEY_HEADS
KEY_COLUMNS = KEY_HEADS * HEAD_SIZE

EPS = 1e-05
NEGATIVE_LARGE = -1e30
EXPONENT = HEAD_SIZE ** (-0.5) * math.log2(math.e)

MESH = pl.DeviceIdType.MESH
HOP, PACE, TWIN_HOP = 3.0, 0.65, 1.0
PASS = {"not_end": (2.85, 4.5, 6.3), "end": (5.0, 5.1, 7.5)}
CROSS = {"not_end": (9.0, 9.1, 10.4), "end": (8.05, 8.15, 11.0)}
WINDOW, LEAD = 4, 7.9
SPLIT, FREE = 0, 3
F32 = jnp.float32
BF16 = jnp.bfloat16


def frequencies():
    index = np.arange(HEAD_SIZE // 2, dtype=np.float64)
    base = 500000.0 ** (-2.0 * index / HEAD_SIZE)
    wave = 2.0 * np.pi / base
    smooth = (8192.0 / wave - 1.0) / 3.0
    blended = (1.0 - smooth) * base / 8.0 + smooth * base
    table = np.where(wave < 2048.0, base, np.where(wave > 8192.0, base / 8.0, blended))
    return np.concatenate([table, table])


def rotary_constants(rows):
    frequency = frequencies()
    sign = np.where(np.arange(HEAD_SIZE) < HEAD_SIZE // 2, -1.0, 1.0)
    angles = np.arange(rows, dtype=np.float64)[:, None] * frequency
    ends = np.ones((8, HEAD_SIZE))
    cosine = np.concatenate([np.cos(angles), ends * frequency])
    sine = np.concatenate([sign * np.sin(angles), ends * sign])
    return np.stack([cosine, sine]).astype(np.float32)


def turn(value, cosine, sine):
    return value * cosine + pltpu.roll(value, HEAD_SIZE // 2, 1) * sine


def scores_of(query, keys):
    return lax.dot_general(query, keys, (((1,), (1,)), ((), ())), preferred_element_type=F32)


def with_ones(values):
    return jnp.concatenate([values, jnp.ones_like(values)], axis=1)


def kernel(
    n_set,
    n_seq,
    pieces,
    hidden_hbm,
    gain_hbm,
    weight_hbm,
    prompt_hbm,
    offset_smem,
    length_smem,
    query_hbm,
    own_hbm,
    rotary_hbm,
    span_out,
    attended_out,
    hidden,
    gain,
    weight,
    prompt,
    query_in,
    own,
    rotary,
    scaled,
    partial,
    sending,
    arriving,
    square_sum,
    square_theirs,
    turns,
    span,
    query,
    best,
    accum,
    load_sem,
    square_send,
    square_recv,
    sum_send,
    sum_recv,
    pz_send,
    pz_recv,
    px_send,
    px_recv,
    pc_send,
    pc_recv,
    sz_send,
    sz_recv,
    sx_send,
    sx_recv,
    sc_send,
    sc_recv,
):
    n_x = n_set // 2
    me_set = lax.axis_index("set")
    me_seq = lax.axis_index("seq")
    me_x, me_core = me_set // 2, me_set % 2
    length, features = hidden.shape
    width = weight.shape[1]
    rows = length // n_seq
    cached = prompt.shape[1] // n_seq
    tokens = query_in.shape[0]
    halves = 2 if width % 512 == 0 else 1
    half = width // halves
    per_set = width // HEAD_SIZE
    per_half = per_set // halves
    part = length // pieces
    chunks = [(j, r) for j in range(per_set) for r in range(pieces)]

    middle = n_seq // 2
    lower = me_seq < middle
    inward = jnp.where(lower, 1, -1)
    inner, outer = me_seq + inward, me_seq - inward
    is_end = jnp.logical_or(me_seq == 0, me_seq == n_seq - 1)
    not_end = jnp.logical_not(is_end)
    is_middle = jnp.logical_or(me_seq == middle - 1, me_seq == middle)
    not_middle = jnp.logical_not(is_middle)
    slot = jnp.where(is_middle, 1, 0)
    has_low, has_high = me_seq > 0, me_seq < n_seq - 1
    twin = me_x * 2 + 1 - me_core

    def set_at(step):
        return ((me_x + step) % n_x) * 2 + me_core

    def twin_at(step):
        return ((me_x + step) % n_x) * 2 + 1 - me_core

    def rows_of(which, count):
        return pl.ds(pl.multiple_of(which * count, count), count)

    loads = []

    def load(source, target):
        copy = pltpu.make_async_copy(source, target, load_sem.at[len(loads)])
        copy.start()
        loads.append(copy)
        return copy

    hidden_load = load(hidden_hbm, hidden)
    gain_load = load(gain_hbm, gain)
    prompt_loads = [
        load(
            prompt_hbm.at[:, pl.ds(s * width, width)],
            prompt.at[s, rows_of(me_seq, cached), :],
        )
        for s in range(n_set)
    ]

    def load_weight(i):
        columns = pl.ds(i * half, half)
        return load(weight_hbm.at[:, columns], weight.at[:, columns])

    weight_loads = [load_weight(0)]

    barrier = pltpu.get_barrier_semaphore()

    def greet(device):
        pl.semaphore_signal(barrier, inc=1, device_id=device, device_id_type=MESH)

    others = range(n_seq - 1)

    def other_seq(j):
        upper = (2 * me_seq) // n_seq
        low = j + (j - me_seq + n_seq) // n_seq
        down = n_seq - 1 - j
        high = down - (me_seq - down + n_seq) // n_seq
        return low + upper * (high - low)

    def ends_at(z):
        return jnp.logical_or(z == 0, z == n_seq - 1)

    for e in range(1, n_x):
        greet({"set": set_at(e)})
    greet({"set": twin})
    for j in others:
        z = other_seq(j)
        sends_here = jnp.logical_or(jnp.logical_not(ends_at(z)), jnp.abs(z - me_seq) == 1)

        @pl.when(sends_here)
        def _(z=z):
            greet({"seq": z})

    waits = []

    def remote(source, target, send_sem, recv_sem, device):
        return pltpu.make_async_remote_copy(
            src_ref=source,
            dst_ref=target,
            send_sem=send_sem,
            recv_sem=recv_sem,
            device_id=device,
            device_id_type=MESH,
        )

    def book(make, when=None):
        waits.append((make, when))

    def start(makes):
        for make in makes:
            make().start()

    def prompt_block(s, z):
        return prompt.at[s, rows_of(z, cached), :]

    def span_block(s, c):
        j, r = chunks[c]
        return span.at[s * per_set + j, pl.ds(r * part, part), :]

    def chunk_of(ref, c):
        j, r = chunks[c]
        return ref.at[j, pl.ds(r * part, part), :]

    def project(i):
        columns = pl.ds(i * half, half)
        product = jnp.dot(scaled[...], weight[:, columns], preferred_element_type=F32)
        for j in range(per_half):
            partial[i * per_half + j] = product[:, j * HEAD_SIZE : (j + 1) * HEAD_SIZE]

    def sum_of(c):
        return lambda: remote(
            chunk_of(sending, c),
            chunk_of(arriving.at[slot], c),
            sum_send.at[c],
            sum_recv.at[slot, c],
            {"seq": inner},
        )

    def square_of():
        return remote(
            square_sum,
            square_theirs.at[slot],
            square_send.at[0],
            square_recv.at[slot],
            {"seq": inner},
        )

    sums = [sum_of(c) for c in range(len(chunks))]
    for c in range(len(chunks)):
        book(sums[c], is_end if c + WINDOW < len(chunks) else None)
    square_copies = [square_of]
    book(square_of)

    def reduce_start(c):
        chunk_of(sending, c)[...] = chunk_of(partial, c)[...].astype(BF16)

    def reduce_more(c):
        come = chunk_of(arriving.at[0], c)
        remote(come, come, sum_send.at[c], sum_recv.at[0, c], {"seq": inner}).wait_recv()
        value = chunk_of(partial, c)[...] + come[...].astype(F32)
        chunk_of(partial, c)[...] = value
        chunk_of(sending, c)[...] = value.astype(BF16)

    def square_more():
        come = square_theirs.at[0]
        remote(come, come, square_send.at[0], square_recv.at[0], {"seq": inner}).wait_recv()
        square_sum[...] += come[...]

    def square_last():
        come = square_theirs.at[1]
        remote(come, come, square_send.at[0], square_recv.at[1], {"seq": inner}).wait_recv()
        total = square_sum[...] + come[...]
        column = jnp.broadcast_to(total[0:1, :], (HEAD_SIZE, length)).T
        inverse = lax.rsqrt(column / MODEL_WIDTH + EPS)
        is_key = me_set * width < KEY_COLUMNS
        cosine, sine = angles_at(0, length)
        turns[0] = jnp.where(is_key, cosine, 1.0) * inverse
        turns[1] = jnp.where(is_key, sine, 0.0) * inverse

    def angles_at(first, count):
        base = rotary.shape[1] - 8
        sign = rotary[1, base : base + 1, :]
        moved = rotary[0, base : base + 1, :] * offset_smem[0].astype(F32)
        cos_moved, sin_moved = jnp.cos(moved), jnp.sin(moved) * sign
        cosine, sine = rotary[0, first : first + count, :], rotary[1, first : first + count, :]
        return (
            cosine * cos_moved - sine * sin_moved,
            sine * cos_moved + cosine * sin_moved,
        )

    def finish(c):
        come = chunk_of(arriving.at[1], c)
        remote(come, come, sum_send.at[c], sum_recv.at[1, c], {"seq": inner}).wait_recv()
        block = chunk_of(partial, c)[...] + come[...].astype(F32)
        r = chunks[c][1]
        cosine, sine = (turns[k, pl.ds(r * part, part), :] for k in range(2))
        span_block(me_set, c)[...] = turn(block, cosine, sine).astype(BF16)

    def receive(c):
        mine = span_block(me_set, c)
        remote(mine, mine, sz_send.at[0], sz_recv.at[c], {"seq": outer}).wait_recv()

    def outward_of(c):
        mine = span_block(me_set, c)
        return lambda: remote(mine, mine, sz_send.at[0], sz_recv.at[c], {"seq": outer})

    def across_of(c, e):
        mine = span_block(me_set, c)
        return lambda: remote(
            mine, mine, sx_send.at[e - 1], sx_recv.at[c, e - 1], {"set": set_at(e)}
        )

    def twin_of(c, e):
        block = span_block(set_at(n_x - e), c)
        return lambda: remote(block, block, sc_send.at[e], sc_recv.at[c, e], {"set": twin})

    def count(make):
        return [make(c) for c in range(len(chunks))]

    def span_set(s):
        return span.at[pl.ds(s * per_set, per_set)]

    outward = count(outward_of)
    across = [count(functools.partial(across_of, e=e)) for e in range(1, n_x)]
    twins = [count(functools.partial(twin_of, e=e)) for e in range(n_x)]
    whole = span_set(me_set)
    book(lambda: remote(whole, whole, sz_send.at[0], sz_recv.at[0], {"seq": outer}), not_end)
    for e in range(1, n_x):
        book(
            functools.partial(
                remote, whole, whole, sx_send.at[e - 1], sx_recv.at[0, e - 1], {"set": twin}
            )
        )
    for e in range(n_x):
        came = span_set(set_at(n_x - e))
        book(
            functools.partial(remote, came, came, sc_send.at[e], sc_recv.at[0, e], {"set": twin})
        )

    def spread(c):
        for copies in across:
            copies[c]().start()
        twins[0][c]().start()

    def cross(c):
        for e in range(1, n_x):
            come = span_block(set_at(n_x - e), c)
            remote(come, come, sx_send.at[e - 1], sx_recv.at[c, e - 1], {"set": twin}).wait_recv()
            twins[e][c]().start()

    def crossed(c):
        for e in range(n_x):
            come = span_block(twin_at(n_x - e), c)
            remote(come, come, sc_send.at[e], sc_recv.at[c, e], {"set": twin}).wait_recv()

    relays = jnp.logical_and(not_end, ends_at(outer))

    def prompt_to(source, z, which):
        block = prompt_block(me_set, source)
        return lambda: remote(
            block, block, pz_send.at[which, z], pz_recv.at[source], {"seq": z}
        )

    def prompt_across(z, e):
        block = prompt_block(me_set, z)
        return lambda: remote(
            block, block, px_send.at[z, e - 1], px_recv.at[z, e - 1], {"set": set_at(e)}
        )

    def prompt_twin(z, e):
        block = prompt_block(set_at(n_x - e), z)
        return lambda: remote(block, block, pc_send.at[z, e], pc_recv.at[z, e], {"set": twin})

    own_prompt, far_prompt = [], []
    for j in others:
        z = other_seq(j)
        reached = jnp.logical_or(not_end, z == inner)
        own_prompt.append((prompt_to(me_seq, z, 0), reached))
        passed = jnp.logical_and(relays, z != outer)
        far_prompt.append((prompt_to(outer, z, 1), passed))
        book(*own_prompt[-1])
        book(*far_prompt[-1])
        for e in range(1, n_x):
            book(prompt_across(z, e))
        for e in range(n_x):
            book(prompt_twin(z, e))

    def send_prompt():
        for make, when in reversed(own_prompt):
            pl.when(when)(lambda make=make: make().start())

    def pass_prompt(j):
        z = other_seq(j)
        block = prompt_block(me_set, z)
        remote(block, block, pz_send.at[0, z], pz_recv.at[z], {"seq": z}).wait_recv()

        @pl.when(jnp.logical_and(relays, z == outer))
        def _():
            for make, when in far_prompt:
                pl.when(when)(lambda make=make: make().start())

        for e in range(1, n_x):
            prompt_across(z, e)().start()
        prompt_twin(z, 0)().start()

    def cross_prompt(j):
        z = other_seq(j)
        for e in range(1, n_x):
            come = prompt_block(set_at(n_x - e), z)
            remote(
                come, come, px_send.at[z, e - 1], px_recv.at[z, e - 1], {"set": twin}
            ).wait_recv()
            prompt_twin(z, e)().start()

    def crossed_prompt(j):
        z = other_seq(j)
        for e in range(n_x):
            come = prompt_block(twin_at(n_x - e), z)
            remote(come, come, pc_send.at[z, e], pc_recv.at[z, e], {"set": twin}).wait_recv()

    def columns_of(head):
        return pl.ds(head * HEAD_SIZE, HEAD_SIZE)

    causal = jnp.concatenate(
        [
            lax.broadcasted_iota(jnp.int32, (tokens, tokens), 0)
            >= lax.broadcasted_iota(jnp.int32, (tokens, tokens), 1)
        ]
        * GROUP,
        axis=0,
    )
    live = lax.broadcasted_iota(jnp.int32, (1, prompt.shape[1]), 1) < offset_smem[0]
    kept = lax.broadcasted_iota(jnp.int32, (tokens, HEAD_SIZE), 0) < length_smem[0]

    def turn_query(head, cosine, sine):
        for g in range(GROUP):
            raw = query_in[:, columns_of(head * GROUP + g)].astype(F32)
            query[head, g * tokens : (g + 1) * tokens, :] = turn(raw, cosine, sine).astype(BF16)

    def attend_own(head, cosine, sine):
        turn_query(head, cosine, sine)
        keys = turn(own[:, columns_of(head)].astype(F32), cosine, sine).astype(BF16)
        values = own[:, columns_of(head + KEY_HEADS)]
        scores = jnp.where(causal, scores_of(query[head], keys), NEGATIVE_LARGE)
        top = jnp.max(scores, axis=1, keepdims=True)
        weights = jnp.exp2((scores - top) * EXPONENT).astype(BF16)
        best[head] = jnp.broadcast_to(top, best.shape[1:])
        accum[head] = jnp.dot(weights, with_ones(values), preferred_element_type=F32)

    def prompt_head(head):
        return prompt[head // per_set, :, columns_of(head % per_set)]

    def attend_more(head, sources):
        parts = []
        for keys, values, mask in sources:
            scores = scores_of(query[head], keys)
            if mask is not None:
                scores = jnp.where(mask, scores, NEGATIVE_LARGE)
            parts.append((scores, values))
        old = best[head]
        top = old
        for scores, _ in parts:
            top = jnp.maximum(top, jnp.max(scores, axis=1, keepdims=True))
        total = accum[head] * jnp.concatenate([jnp.exp2((old - top) * EXPONENT)] * 2, axis=1)
        for scores, values in parts:
            spread_top = jnp.concatenate([top] * (scores.shape[1] // HEAD_SIZE), axis=1)
            weights = jnp.exp2((scores - spread_top) * EXPONENT).astype(BF16)
            total += jnp.dot(weights, with_ones(values), preferred_element_type=F32)
        return top, total

    def prompt_source(head):
        return prompt_head(head), prompt_head(head + KEY_HEADS), live

    def attend_prompt(head):
        top, total = attend_more(head, [prompt_source(head)])
        best[head] = top
        accum[head] = total

    def attend_last(head, with_prompt):
        sources = [(span[head], span[head + KEY_HEADS], None)]
        if with_prompt:
            sources = [prompt_source(head)] + sources
        _, total = attend_more(head, sources)
        mixed = total[:, :HEAD_SIZE] / total[:, HEAD_SIZE:]
        for g in range(GROUP):
            column = (head * GROUP + g) * HEAD_SIZE
            attended_out[:, column : column + HEAD_SIZE] = jnp.where(
                kept, mixed[g * tokens : (g + 1) * tokens, :], 0.0
            ).astype(BF16)

    hidden_load.wait()
    gain_load.wait()
    squares = jnp.zeros((length, HEAD_SIZE), F32)
    for i in range(features // HEAD_SIZE):
        block = hidden[:, i * HEAD_SIZE : (i + 1) * HEAD_SIZE]
        wide = block.astype(F32)
        squares += wide * wide
        scaled[:, i * HEAD_SIZE : (i + 1) * HEAD_SIZE] = block * gain[i : i + 1, :]
    turns[0] = squares
    for copy in prompt_loads:
        copy.wait()
    weight_loads.extend(load_weight(i) for i in range(1, halves))
    rotary_load = load(rotary_hbm, rotary)
    own_load = load(own_hbm.at[0], own)
    query_load = load(query_hbm.at[0], query_in)
    def meet():
        lines = jnp.where(is_end, 1, n_seq - 1)
        pl.semaphore_wait(barrier, n_x + lines)
        send_prompt()

    pl.when(is_end)(meet)
    weight_loads[0].wait()
    project(0)

    hop, pace, twin_hop = HOP, PACE, TWIN_HOP
    n_chunks = len(chunks)
    final = hop + pace * LEAD
    agenda = []

    def at(time, do, who=None):
        agenda.append((time, len(agenda), who, do))

    def start_sum(c):
        reduce_start(c)
        sums[c]().start()

    def project_rest():
        for i in range(1, halves):
            weight_loads[i].wait()
            project(i)

    def sum_squares():
        square_row = jnp.sum(turns[0].T, axis=0, keepdims=True)
        square_sum[...] = jnp.broadcast_to(square_row, square_sum.shape)

    def more_sum(c):
        reduce_more(c)
        if c >= WINDOW:
            sums[c - WINDOW]().wait_send()
        sums[c]().start()

    def more_square():
        square_more()
        start(square_copies)

    def finish_one(c):
        finish(c)
        pl.when(not_end)(lambda: outward[c]().start())
        spread(c)

    def receive_one(c):
        receive(c)
        pl.when(not_end)(lambda: outward[c]().start())
        spread(c)

    def ready_for_own():
        rotary_load.wait()
        own_load.wait()
        query_load.wait()

    def own_heads(heads):
        own_cosine, own_sine = angles_at(length, tokens)
        for head in heads:
            attend_own(head, own_cosine, own_sine)

    def store_span():
        for j in range(per_set):
            span_out[:, columns_of(j)] = span[me_set * per_set + j, rows_of(me_seq, rows), :]

    own_time, project_time = 0.33, 0.8
    at(project_time + 0.05, meet, "not_end")
    at(0.1, sum_squares)
    at(0.15, lambda: start(square_copies), "end")
    at(0.2, project_rest)
    for c in range(n_chunks):
        when = 0.05 * c if c < per_half * pieces // 2 else project_time + pace * (c - 2)
        at(when, functools.partial(start_sum, c), "end")
    at(project_time, ready_for_own)
    for head in range(0, KEY_HEADS, 2):
        heads = range(head, head + 2)
        at(project_time + own_time * (head + 0.5), functools.partial(own_heads, heads))
    for c in range(n_chunks):
        at(hop + pace * c, functools.partial(more_sum, c), "not_end")
        at(final + pace * c + 0.005, functools.partial(finish_one, c), "middle")
        at(final + hop + pace * c, functools.partial(cross, c), "middle")
        at(final + hop + pace * c, functools.partial(receive_one, c), "not_middle")
        at(final + 2 * hop + pace * c, functools.partial(cross, c), "not_middle")
    at(hop + 0.01, more_square, "not_end")
    at(final, square_last, "middle")

    for j in others:
        step = min(2, j * 3 // (n_seq - 1))
        for who in ("not_end", "end"):
            at(PASS[who][step], functools.partial(pass_prompt, j), who)
            at(CROSS[who][step], functools.partial(cross_prompt, j), who)

    def all_prompt():
        for j in others:
            crossed_prompt(j)

    def prompt_heads(heads):
        for head in heads:
            attend_prompt(head)

    groups = [[h for h in range(KEY_HEADS) if h % per_set == j] for j in range(per_set)]
    split = min(SPLIT, per_set)
    free = final + hop + pace * FREE + 0.02
    at(free, all_prompt)
    for k in range(split, per_set):
        at(free + 0.01 + pace * (k - split), functools.partial(prompt_heads, groups[k]))
    for j in range(per_set):
        arrived = final + 2 * hop + pace * ((j + 1) * pieces - 1) + twin_hop
        if j + 1 == per_set:
            at(arrived - 0.5, store_span)

        def last_heads(j=j):
            for r in range(pieces):
                crossed(j * pieces + r)
            for head in groups[j]:
                attend_last(head, j < split)

        at(arrived, last_heads)

    who_is = {
        "end": is_end,
        "not_end": not_end,
        "middle": is_middle,
        "not_middle": not_middle,
    }
    agenda.sort(key=lambda entry: entry[:2])
    while agenda:
        time, _, who, _ = agenda[0]
        group = []
        while agenda and agenda[0][2] == who and (who is not None or not group):
            group.append(agenda.pop(0)[3])

        def run(group=group):
            for do in group:
                do()

        if who is None:
            run()
        else:
            pl.when(who_is[who])(run)

    for make, when in waits:
        if when is None:
            make().wait_send()
        else:
            pl.when(when)(lambda make=make: make().wait_send())


def hand_on(span_in, attended_in, span_out, attended_out, sem):
    copies = [
        pltpu.make_async_copy(attended_in, attended_out.at[0], sem.at[0]),
        pltpu.make_async_copy(span_in, span_out, sem.at[1]),
    ]
    for copy in copies:
        copy.start()
    for copy in copies:
        copy.wait()


def on_device(
    n_set,
    n_seq,
    span_hidden,
    norm_gain,
    key_value_weight,
    prompt_key_value,
    span_offset,
    cont_query,
    continuation_key_value,
    cont_lengths,
):
    length, features = span_hidden.shape
    width = key_value_weight.shape[1]
    rows = length // n_seq
    cached = prompt_key_value.shape[0]
    tokens = cont_query.shape[1]
    n_x = n_set // 2
    halves = 2 if width % 512 == 0 else 1
    pieces = 2
    per_set = width // HEAD_SIZE
    blocks = n_set * per_set
    chunks = per_set * pieces
    rotary = jnp.asarray(rotary_constants(length + tokens))
    gain = norm_gain.reshape(features // HEAD_SIZE, HEAD_SIZE)
    dma = pltpu.SemaphoreType.DMA
    anywhere = pl.BlockSpec(memory_space=pl.ANY)
    in_vmem = pl.BlockSpec(memory_space=pltpu.VMEM)
    in_smem = pl.BlockSpec(memory_space=pltpu.SMEM)

    def far(array):
        return pltpu.with_memory_space_constraint(array, pltpu.HBM)

    span_rows, attended = pl.pallas_call(
        functools.partial(kernel, n_set, n_seq, pieces),
        out_shape=(
            pltpu.VMEM((rows, width), BF16),
            pltpu.VMEM((tokens, QUERY_HEADS * HEAD_SIZE), BF16),
        ),
        in_specs=[
            anywhere,
            anywhere,
            anywhere,
            anywhere,
            in_smem,
            in_smem,
            anywhere,
            anywhere,
            anywhere,
        ],
        out_specs=(in_vmem, in_vmem),
        scratch_shapes=[
            pltpu.VMEM((length, features), BF16),
            pltpu.VMEM((features // HEAD_SIZE, HEAD_SIZE), BF16),
            pltpu.VMEM((features, width), BF16),
            pltpu.VMEM((n_set, cached * n_seq, width), BF16),
            pltpu.VMEM((tokens, QUERY_HEADS * HEAD_SIZE), BF16),
            pltpu.VMEM((tokens, 2 * KEY_COLUMNS), BF16),
            pltpu.VMEM(rotary.shape, F32),
            pltpu.VMEM((length, features), BF16),
            pltpu.VMEM((per_set, length, HEAD_SIZE), F32),
            pltpu.VMEM((per_set, length, HEAD_SIZE), BF16),
            pltpu.VMEM((2, per_set, length, HEAD_SIZE), BF16),
            pltpu.VMEM((8, length), F32),
            pltpu.VMEM((2, 8, length), F32),
            pltpu.VMEM((2, length, HEAD_SIZE), F32),
            pltpu.VMEM((blocks, length, HEAD_SIZE), BF16),
            pltpu.VMEM((KEY_HEADS, GROUP * tokens, HEAD_SIZE), BF16),
            pltpu.VMEM((KEY_HEADS, GROUP * tokens, HEAD_SIZE), F32),
            pltpu.VMEM((KEY_HEADS, GROUP * tokens, 2 * HEAD_SIZE), F32),
            dma((n_set + halves + 5,)),
            dma((1,)),
            dma((2,)),
            dma((chunks,)),
            dma((2, chunks)),
            dma((2, n_seq)),
            dma((n_seq,)),
            dma((n_seq, n_x - 1)),
            dma((n_seq, n_x - 1)),
            dma((n_seq, n_x)),
            dma((n_seq, n_x)),
            dma((1,)),
            dma((chunks,)),
            dma((n_x - 1,)),
            dma((chunks, n_x - 1)),
            dma((n_x,)),
            dma((chunks, n_x)),
        ],
        compiler_params=pltpu.CompilerParams(
            collective_id=0, has_side_effects=True, vmem_limit_bytes=40 << 20
        ),
        name="project_gather_attend",
    )(
        far(span_hidden),
        far(gain),
        far(key_value_weight),
        far(prompt_key_value),
        span_offset,
        cont_lengths,
        far(cont_query),
        far(continuation_key_value),
        far(rotary),
    )
    return pl.pallas_call(
        hand_on,
        out_shape=(
            jax.ShapeDtypeStruct((rows, width), BF16),
            jax.ShapeDtypeStruct((1, tokens, QUERY_HEADS * HEAD_SIZE), BF16),
        ),
        in_specs=[anywhere, anywhere],
        out_specs=(anywhere, anywhere),
        scratch_shapes=[dma((2,))],
        compiler_params=pltpu.CompilerParams(vmem_limit_bytes=1 << 20),
        name="hand_on",
    )(span_rows, attended)


def solution(mesh):
    placed = (
        P("parts", "seq"),
        P("seq"),
        P("seq", "set"),
        P(("parts", "seq"), None),
        P("parts"),
        P(("parts", "set", "seq"), None, None),
        P(("parts", "set", "seq"), None, None),
        P(("parts", "set", "seq")),
    )
    return jax.shard_map(
        functools.partial(on_device, mesh.shape["set"], mesh.shape["seq"]),
        mesh=mesh,
        in_specs=placed,
        out_specs=(P(("parts", "seq"), "set"), P(("parts", "set", "seq"), None, None)),
        check_vma=False,
    )
```

```python
import functools
import math

import jax
import jax.numpy as jnp
import numpy as np
from jax import lax
from jax.experimental import pallas as pl
from jax.experimental.pallas import tpu as pltpu
from jax.sharding import PartitionSpec as P

MODEL_WIDTH = 8192
QUERY_HEADS = 64
KEY_HEADS = 8
HEAD_SIZE = 128
GROUP = QUERY_HEADS // KEY_HEADS
KEY_COLUMNS = KEY_HEADS * HEAD_SIZE

EPS = 1e-05
NEGATIVE_LARGE = -1e30
EXPONENT = HEAD_SIZE ** (-0.5) * math.log2(math.e)

MESH = pl.DeviceIdType.MESH
HOP, PACE, TWIN_HOP = 3.0, 0.65, 1.0
PASS = {"not_end": (2.85, 4.5, 6.3), "end": (5.0, 5.1, 7.5)}
CROSS = {"not_end": (9.0, 9.1, 10.4), "end": (8.05, 8.15, 11.0)}
WINDOW, LEAD = 4, 7.9
SPLIT, FREE = 0, 3
F32 = jnp.float32
BF16 = jnp.bfloat16


def frequencies():
    index = np.arange(HEAD_SIZE // 2, dtype=np.float64)
    base = 500000.0 ** (-2.0 * index / HEAD_SIZE)
    wave = 2.0 * np.pi / base
    smooth = (8192.0 / wave - 1.0) / 3.0
    blended = (1.0 - smooth) * base / 8.0 + smooth * base
    table = np.where(wave < 2048.0, base, np.where(wave > 8192.0, base / 8.0, blended))
    return np.concatenate([table, table])


def rotary_constants(rows):
    frequency = frequencies()
    sign = np.where(np.arange(HEAD_SIZE) < HEAD_SIZE // 2, -1.0, 1.0)
    angles = np.arange(rows, dtype=np.float64)[:, None] * frequency
    ends = np.ones((8, HEAD_SIZE))
    cosine = np.concatenate([np.cos(angles), ends * frequency])
    sine = np.concatenate([sign * np.sin(angles), ends * sign])
    return np.stack([cosine, sine]).astype(np.float32)


def turn(value, cosine, sine):
    return value * cosine + pltpu.roll(value, HEAD_SIZE // 2, 1) * sine


def scores_of(query, keys):
    return lax.dot_general(query, keys, (((1,), (1,)), ((), ())), preferred_element_type=F32)


def with_ones(values):
    return jnp.concatenate([values, jnp.ones_like(values)], axis=1)


def kernel(
    n_set,
    n_seq,
    pieces,
    hidden_hbm,
    gain_hbm,
    weight_hbm,
    prompt_hbm,
    offset_smem,
    length_smem,
    query_hbm,
    own_hbm,
    rotary_hbm,
    span_out,
    attended_out,
    hidden,
    gain,
    weight,
    prompt,
    query_in,
    own,
    rotary,
    scaled,
    partial,
    sending,
    arriving,
    square_sum,
    square_theirs,
    turns,
    span,
    query,
    best,
    accum,
    load_sem,
    square_send,
    square_recv,
    sum_send,
    sum_recv,
    pz_send,
    pz_recv,
    px_send,
    px_recv,
    pc_send,
    pc_recv,
    sz_send,
    sz_recv,
    sx_send,
    sx_recv,
    sc_send,
    sc_recv,
):
    n_x = n_set // 2
    me_set = lax.axis_index("set")
    me_seq = lax.axis_index("seq")
    me_x, me_core = me_set // 2, me_set % 2
    length, features = hidden.shape
    width = weight.shape[1]
    rows = length // n_seq
    cached = prompt.shape[1] // n_seq
    tokens = query_in.shape[0]
    halves = 2 if width % 512 == 0 else 1
    half = width // halves
    per_set = width // HEAD_SIZE
    per_half = per_set // halves
    part = length // pieces
    chunks = [(j, r) for j in range(per_set) for r in range(pieces)]

    middle = n_seq // 2
    lower = me_seq < middle
    inward = jnp.where(lower, 1, -1)
    inner, outer = me_seq + inward, me_seq - inward
    is_end = jnp.logical_or(me_seq == 0, me_seq == n_seq - 1)
    not_end = jnp.logical_not(is_end)
    is_middle = jnp.logical_or(me_seq == middle - 1, me_seq == middle)
    not_middle = jnp.logical_not(is_middle)
    slot = jnp.where(is_middle, 1, 0)
    has_low, has_high = me_seq > 0, me_seq < n_seq - 1
    twin = me_x * 2 + 1 - me_core

    def set_at(step):
        return ((me_x + step) % n_x) * 2 + me_core

    def twin_at(step):
        return ((me_x + step) % n_x) * 2 + 1 - me_core

    def rows_of(which, count):
        return pl.ds(pl.multiple_of(which * count, count), count)

    loads = []

    def load(source, target):
        copy = pltpu.make_async_copy(source, target, load_sem.at[len(loads)])
        copy.start()
        loads.append(copy)
        return copy

    hidden_load = load(hidden_hbm, hidden)
    gain_load = load(gain_hbm, gain)
    prompt_sem = load_sem.at[len(loads)]
    for s in range(n_set):
        pltpu.make_async_copy(
            prompt_hbm.at[:, pl.ds(s * width, width)],
            prompt.at[s, rows_of(me_seq, cached), :],
            prompt_sem,
        ).start()
    landed = prompt.at[:, rows_of(me_seq, cached), :]
    loads.append(pltpu.make_async_copy(landed, landed, prompt_sem))
    prompt_loads = [loads[-1]]

    def load_weight(i):
        columns = pl.ds(i * half, half)
        return load(weight_hbm.at[:, columns], weight.at[:, columns])

    weight_loads = [load_weight(0)]

    barrier = pltpu.get_barrier_semaphore()

    def greet(device):
        pl.semaphore_signal(barrier, inc=1, device_id=device, device_id_type=MESH)

    others = range(n_seq - 1)

    def other_seq(j):
        upper = (2 * me_seq) // n_seq
        low = j + (j - me_seq + n_seq) // n_seq
        down = n_seq - 1 - j
        high = down - (me_seq - down + n_seq) // n_seq
        return low + upper * (high - low)

    def ends_at(z):
        return jnp.logical_or(z == 0, z == n_seq - 1)

    for e in range(1, n_x):
        greet({"set": set_at(e)})
    greet({"set": twin})
    for j in others:
        z = other_seq(j)
        sends_here = jnp.logical_or(jnp.logical_not(ends_at(z)), jnp.abs(z - me_seq) == 1)

        @pl.when(sends_here)
        def _(z=z):
            greet({"seq": z})

    waits = []

    def remote(source, target, send_sem, recv_sem, device):
        return pltpu.make_async_remote_copy(
            src_ref=source,
            dst_ref=target,
            send_sem=send_sem,
            recv_sem=recv_sem,
            device_id=device,
            device_id_type=MESH,
        )

    def book(make, when=None):
        waits.append((make, when))

    def start(makes):
        for make in makes:
            make().start()

    def prompt_block(s, z):
        return prompt.at[s, rows_of(z, cached), :]

    def span_block(s, c):
        j, r = chunks[c]
        return span.at[s * per_set + j, pl.ds(r * part, part), :]

    def chunk_of(ref, c):
        j, r = chunks[c]
        return ref.at[j, pl.ds(r * part, part), :]

    def project(i):
        columns = pl.ds(i * half, half)
        product = jnp.dot(scaled[...], weight[:, columns], preferred_element_type=F32)
        for j in range(per_half):
            partial[i * per_half + j] = product[:, j * HEAD_SIZE : (j + 1) * HEAD_SIZE]

    def sum_of(c):
        return lambda: remote(
            chunk_of(sending, c),
            chunk_of(arriving.at[slot], c),
            sum_send.at[c],
            sum_recv.at[slot, c],
            {"seq": inner},
        )

    def square_of():
        return remote(
            square_sum,
            square_theirs.at[slot],
            square_send.at[0],
            square_recv.at[slot],
            {"seq": inner},
        )

    sums = [sum_of(c) for c in range(len(chunks))]
    for c in range(len(chunks)):
        book(sums[c], is_end if c + WINDOW < len(chunks) else None)
    square_copies = [square_of]
    book(square_of)

    def reduce_start(c):
        chunk_of(sending, c)[...] = chunk_of(partial, c)[...].astype(BF16)

    def reduce_more(c):
        come = chunk_of(arriving.at[0], c)
        remote(come, come, sum_send.at[c], sum_recv.at[0, c], {"seq": inner}).wait_recv()
        value = chunk_of(partial, c)[...] + come[...].astype(F32)
        chunk_of(partial, c)[...] = value
        chunk_of(sending, c)[...] = value.astype(BF16)

    def square_more():
        come = square_theirs.at[0]
        remote(come, come, square_send.at[0], square_recv.at[0], {"seq": inner}).wait_recv()
        square_sum[...] += come[...]

    def square_last():
        come = square_theirs.at[1]
        remote(come, come, square_send.at[0], square_recv.at[1], {"seq": inner}).wait_recv()
        total = square_sum[...] + come[...]
        column = jnp.broadcast_to(total[0:1, :], (HEAD_SIZE, length)).T
        inverse = lax.rsqrt(column / MODEL_WIDTH + EPS)
        is_key = me_set * width < KEY_COLUMNS
        cosine, sine = angles_at(0, length)
        turns[0] = jnp.where(is_key, cosine, 1.0) * inverse
        turns[1] = jnp.where(is_key, sine, 0.0) * inverse

    def angles_at(first, count):
        base = rotary.shape[1] - 8
        sign = rotary[1, base : base + 1, :]
        moved = rotary[0, base : base + 1, :] * offset_smem[0].astype(F32)
        cos_moved, sin_moved = jnp.cos(moved), jnp.sin(moved) * sign
        cosine, sine = rotary[0, first : first + count, :], rotary[1, first : first + count, :]
        return (
            cosine * cos_moved - sine * sin_moved,
            sine * cos_moved + cosine * sin_moved,
        )

    def finish(c):
        come = chunk_of(arriving.at[1], c)
        remote(come, come, sum_send.at[c], sum_recv.at[1, c], {"seq": inner}).wait_recv()
        block = chunk_of(partial, c)[...] + come[...].astype(F32)
        r = chunks[c][1]
        cosine, sine = (turns[k, pl.ds(r * part, part), :] for k in range(2))
        span_block(me_set, c)[...] = turn(block, cosine, sine).astype(BF16)

    def receive(c):
        mine = span_block(me_set, c)
        remote(mine, mine, sz_send.at[0], sz_recv.at[c], {"seq": outer}).wait_recv()

    def outward_of(c):
        mine = span_block(me_set, c)
        return lambda: remote(mine, mine, sz_send.at[0], sz_recv.at[c], {"seq": outer})

    def across_of(c, e):
        mine = span_block(me_set, c)
        return lambda: remote(
            mine, mine, sx_send.at[e - 1], sx_recv.at[c, e - 1], {"set": set_at(e)}
        )

    def twin_of(c, e):
        block = span_block(set_at(n_x - e), c)
        return lambda: remote(block, block, sc_send.at[e], sc_recv.at[chunks[c][0], e], {"set": twin})

    def count(make):
        return [make(c) for c in range(len(chunks))]

    def span_set(s):
        return span.at[pl.ds(s * per_set, per_set)]

    outward = count(outward_of)
    across = [count(functools.partial(across_of, e=e)) for e in range(1, n_x)]
    twins = [count(functools.partial(twin_of, e=e)) for e in range(n_x)]
    whole = span_set(me_set)
    book(lambda: remote(whole, whole, sz_send.at[0], sz_recv.at[0], {"seq": outer}), not_end)
    for e in range(1, n_x):
        book(
            functools.partial(
                remote, whole, whole, sx_send.at[e - 1], sx_recv.at[0, e - 1], {"set": twin}
            )
        )
    for e in range(n_x):
        came = span_set(set_at(n_x - e))
        book(
            functools.partial(remote, came, came, sc_send.at[e], sc_recv.at[0, e], {"set": twin})
        )

    def spread(c):
        for copies in across:
            copies[c]().start()
        twins[0][c]().start()

    def cross(c):
        for e in range(1, n_x):
            come = span_block(set_at(n_x - e), c)
            remote(come, come, sx_send.at[e - 1], sx_recv.at[c, e - 1], {"set": twin}).wait_recv()
            twins[e][c]().start()

    def crossed(j):
        for e in range(n_x):
            come = span.at[twin_at(n_x - e) * per_set + j]
            remote(come, come, sc_send.at[e], sc_recv.at[j, e], {"set": twin}).wait_recv()

    relays = jnp.logical_and(not_end, ends_at(outer))

    def prompt_to(source, z, which):
        block = prompt_block(me_set, source)
        return lambda: remote(
            block, block, pz_send.at[which, z], pz_recv.at[source], {"seq": z}
        )

    def prompt_across(z, e):
        block = prompt_block(me_set, z)
        return lambda: remote(
            block, block, px_send.at[e - 1], px_recv.at[z, e - 1], {"set": set_at(e)}
        )

    def prompt_twin(z, e):
        block = prompt_block(set_at(n_x - e), z)
        return lambda: remote(block, block, pc_send.at[e], pc_recv.at[e], {"set": twin})

    own_prompt, far_prompt = [], []
    for j in others:
        z = other_seq(j)
        reached = jnp.logical_or(not_end, z == inner)
        own_prompt.append((prompt_to(me_seq, z, 0), reached))
        passed = jnp.logical_and(relays, z != outer)
        far_prompt.append((prompt_to(outer, z, 1), passed))
        book(*own_prompt[-1])
        book(*far_prompt[-1])

    def all_blocks(s):
        return prompt.at[s, pl.ds(0, (n_seq - 1) * cached), :]

    sent = all_blocks(me_set)
    for e in range(1, n_x):
        book(
            functools.partial(
                remote, sent, sent, px_send.at[e - 1], px_recv.at[0, e - 1], {"set": twin}
            )
        )
    for e in range(n_x):
        book(functools.partial(remote, sent, sent, pc_send.at[e], pc_recv.at[e], {"set": twin}))

    def send_prompt():
        for make, when in reversed(own_prompt):
            pl.when(when)(lambda make=make: make().start())

    def pass_prompt(j):
        z = other_seq(j)
        block = prompt_block(me_set, z)
        remote(block, block, pz_send.at[0, z], pz_recv.at[z], {"seq": z}).wait_recv()

        @pl.when(jnp.logical_and(relays, z == outer))
        def _():
            for make, when in far_prompt:
                pl.when(when)(lambda make=make: make().start())

        for e in range(1, n_x):
            prompt_across(z, e)().start()
        prompt_twin(z, 0)().start()

    def cross_prompt(j):
        z = other_seq(j)
        for e in range(1, n_x):
            come = prompt_block(set_at(n_x - e), z)
            remote(
                come, come, px_send.at[e - 1], px_recv.at[z, e - 1], {"set": twin}
            ).wait_recv()
            prompt_twin(z, e)().start()

    def crossed_prompt():
        for e in range(n_x):
            come = all_blocks(twin_at(n_x - e))
            remote(come, come, pc_send.at[e], pc_recv.at[e], {"set": twin}).wait_recv()

    def columns_of(head):
        return pl.ds(head * HEAD_SIZE, HEAD_SIZE)

    causal = jnp.concatenate(
        [
            lax.broadcasted_iota(jnp.int32, (tokens, tokens), 0)
            >= lax.broadcasted_iota(jnp.int32, (tokens, tokens), 1)
        ]
        * GROUP,
        axis=0,
    )
    live = lax.broadcasted_iota(jnp.int32, (1, prompt.shape[1]), 1) < offset_smem[0]
    kept = lax.broadcasted_iota(jnp.int32, (tokens, HEAD_SIZE), 0) < length_smem[0]

    def turn_query(head, cosine, sine):
        for g in range(GROUP):
            raw = query_in[:, columns_of(head * GROUP + g)].astype(F32)
            query[head, g * tokens : (g + 1) * tokens, :] = turn(raw, cosine, sine).astype(BF16)

    def attend_own(head, cosine, sine):
        turn_query(head, cosine, sine)
        keys = turn(own[:, columns_of(head)].astype(F32), cosine, sine).astype(BF16)
        values = own[:, columns_of(head + KEY_HEADS)]
        scores = jnp.where(causal, scores_of(query[head], keys), NEGATIVE_LARGE)
        top = jnp.max(scores, axis=1, keepdims=True)
        weights = jnp.exp2((scores - top) * EXPONENT).astype(BF16)
        best[head] = jnp.broadcast_to(top, best.shape[1:])
        accum[head] = jnp.dot(weights, with_ones(values), preferred_element_type=F32)

    def prompt_head(head):
        return prompt[head // per_set, :, columns_of(head % per_set)]

    def attend_more(head, sources):
        parts = []
        for keys, values, mask in sources:
            scores = scores_of(query[head], keys)
            if mask is not None:
                scores = jnp.where(mask, scores, NEGATIVE_LARGE)
            parts.append((scores, values))
        old = best[head]
        top = old
        for scores, _ in parts:
            top = jnp.maximum(top, jnp.max(scores, axis=1, keepdims=True))
        total = accum[head] * jnp.concatenate([jnp.exp2((old - top) * EXPONENT)] * 2, axis=1)
        for scores, values in parts:
            spread_top = jnp.concatenate([top] * (scores.shape[1] // HEAD_SIZE), axis=1)
            weights = jnp.exp2((scores - spread_top) * EXPONENT).astype(BF16)
            total += jnp.dot(weights, with_ones(values), preferred_element_type=F32)
        return top, total

    def prompt_source(head):
        return prompt_head(head), prompt_head(head + KEY_HEADS), live

    def attend_prompt(head):
        top, total = attend_more(head, [prompt_source(head)])
        best[head] = top
        accum[head] = total

    def attend_last(head, with_prompt):
        sources = [(span[head], span[head + KEY_HEADS], None)]
        if with_prompt:
            sources = [prompt_source(head)] + sources
        _, total = attend_more(head, sources)
        mixed = total[:, :HEAD_SIZE] / total[:, HEAD_SIZE:]
        for g in range(GROUP):
            column = (head * GROUP + g) * HEAD_SIZE
            attended_out[:, column : column + HEAD_SIZE] = jnp.where(
                kept, mixed[g * tokens : (g + 1) * tokens, :], 0.0
            ).astype(BF16)

    hidden_load.wait()
    gain_load.wait()
    squares = jnp.zeros((length, HEAD_SIZE), F32)
    for i in range(features // HEAD_SIZE):
        block = hidden[:, i * HEAD_SIZE : (i + 1) * HEAD_SIZE]
        wide = block.astype(F32)
        squares += wide * wide
        scaled[:, i * HEAD_SIZE : (i + 1) * HEAD_SIZE] = block * gain[i : i + 1, :]
    turns[0] = squares
    for copy in prompt_loads:
        copy.wait()
    weight_loads.extend(load_weight(i) for i in range(1, halves))
    rotary_load = load(rotary_hbm, rotary)
    own_load = load(own_hbm.at[0], own)
    query_load = load(query_hbm.at[0], query_in)
    def meet():
        lines = jnp.where(is_end, 1, n_seq - 1)
        pl.semaphore_wait(barrier, n_x + lines)
        send_prompt()

    pl.when(is_end)(meet)
    weight_loads[0].wait()
    project(0)

    hop, pace, twin_hop = HOP, PACE, TWIN_HOP
    n_chunks = len(chunks)
    final = hop + pace * LEAD
    agenda = []

    def at(time, do, who=None):
        agenda.append((time, len(agenda), who, do))

    def start_sum(c):
        reduce_start(c)
        sums[c]().start()

    def project_rest():
        for i in range(1, halves):
            weight_loads[i].wait()
            project(i)

    def sum_squares():
        square_row = jnp.sum(turns[0].T, axis=0, keepdims=True)
        square_sum[...] = jnp.broadcast_to(square_row, square_sum.shape)

    def more_sum(c):
        reduce_more(c)
        if c >= WINDOW:
            sums[c - WINDOW]().wait_send()
        sums[c]().start()

    def more_square():
        square_more()
        start(square_copies)

    def finish_one(c):
        finish(c)
        pl.when(not_end)(lambda: outward[c]().start())
        spread(c)

    def receive_one(c):
        receive(c)
        pl.when(not_end)(lambda: outward[c]().start())
        spread(c)

    def ready_for_own():
        rotary_load.wait()
        own_load.wait()
        query_load.wait()

    def own_heads(heads):
        own_cosine, own_sine = angles_at(length, tokens)
        for head in heads:
            attend_own(head, own_cosine, own_sine)

    def store_span():
        for j in range(per_set):
            span_out[:, columns_of(j)] = span[me_set * per_set + j, rows_of(me_seq, rows), :]

    own_time, project_time = 0.33, 0.8
    at(project_time + 0.05, meet, "not_end")
    at(0.1, sum_squares)
    at(0.15, lambda: start(square_copies), "end")
    at(0.2, project_rest)
    for c in range(n_chunks):
        when = 0.05 * c if c < per_half * pieces // 2 else project_time + pace * (c - 2)
        at(when, functools.partial(start_sum, c), "end")
    at(project_time, ready_for_own)
    for head in range(0, KEY_HEADS, 2):
        heads = range(head, head + 2)
        at(project_time + own_time * (head + 0.5), functools.partial(own_heads, heads))
    for c in range(n_chunks):
        at(hop + pace * c, functools.partial(more_sum, c), "not_end")
        at(final + pace * c + 0.005, functools.partial(finish_one, c), "middle")
        at(final + hop + pace * c, functools.partial(cross, c), "middle")
        at(final + hop + pace * c, functools.partial(receive_one, c), "not_middle")
        at(final + 2 * hop + pace * c, functools.partial(cross, c), "not_middle")
    at(hop + 0.01, more_square, "not_end")
    at(final, square_last, "middle")

    for j in others:
        step = min(2, j * 3 // (n_seq - 1))
        for who in ("not_end", "end"):
            at(PASS[who][step], functools.partial(pass_prompt, j), who)
            at(CROSS[who][step], functools.partial(cross_prompt, j), who)

    def prompt_heads(heads):
        for head in heads:
            attend_prompt(head)

    groups = [[h for h in range(KEY_HEADS) if h % per_set == j] for j in range(per_set)]
    split = min(SPLIT, per_set)
    free = final + hop + pace * FREE + 0.02
    at(free, crossed_prompt)
    for k in range(split, per_set):
        at(free + 0.01 + pace * (k - split), functools.partial(prompt_heads, groups[k]))
    for j in range(per_set):
        arrived = final + 2 * hop + pace * ((j + 1) * pieces - 1) + twin_hop
        if j + 1 == per_set:
            at(arrived - 0.5, store_span)

        def last_heads(j=j):
            crossed(j)
            for head in groups[j]:
                attend_last(head, j < split)

        at(arrived, last_heads)

    who_is = {
        "end": is_end,
        "not_end": not_end,
        "middle": is_middle,
        "not_middle": not_middle,
    }
    agenda.sort(key=lambda entry: entry[:2])
    while agenda:
        time, _, who, _ = agenda[0]
        group = []
        while agenda and agenda[0][2] == who and (who is not None or not group):
            group.append(agenda.pop(0)[3])

        def run(group=group):
            for do in group:
                do()

        if who is None:
            run()
        else:
            pl.when(who_is[who])(run)

    for make, when in waits:
        if when is None:
            make().wait_send()
        else:
            pl.when(when)(lambda make=make: make().wait_send())


def hand_on(span_in, attended_in, span_out, attended_out, sem):
    copies = [
        pltpu.make_async_copy(attended_in, attended_out.at[0], sem.at[0]),
        pltpu.make_async_copy(span_in, span_out, sem.at[1]),
    ]
    for copy in copies:
        copy.start()
    for copy in copies:
        copy.wait()


def on_device(
    n_set,
    n_seq,
    span_hidden,
    norm_gain,
    key_value_weight,
    prompt_key_value,
    span_offset,
    cont_query,
    continuation_key_value,
    cont_lengths,
):
    length, features = span_hidden.shape
    width = key_value_weight.shape[1]
    rows = length // n_seq
    cached = prompt_key_value.shape[0]
    tokens = cont_query.shape[1]
    n_x = n_set // 2
    halves = 2 if width % 512 == 0 else 1
    pieces = 2
    per_set = width // HEAD_SIZE
    blocks = n_set * per_set
    chunks = per_set * pieces
    rotary = jnp.asarray(rotary_constants(length + tokens))
    gain = norm_gain.reshape(features // HEAD_SIZE, HEAD_SIZE)
    dma = pltpu.SemaphoreType.DMA
    anywhere = pl.BlockSpec(memory_space=pl.ANY)
    in_vmem = pl.BlockSpec(memory_space=pltpu.VMEM)
    in_smem = pl.BlockSpec(memory_space=pltpu.SMEM)

    def far(array):
        return pltpu.with_memory_space_constraint(array, pltpu.HBM)

    span_rows, attended = pl.pallas_call(
        functools.partial(kernel, n_set, n_seq, pieces),
        out_shape=(
            pltpu.VMEM((rows, width), BF16),
            pltpu.VMEM((tokens, QUERY_HEADS * HEAD_SIZE), BF16),
        ),
        in_specs=[
            anywhere,
            anywhere,
            anywhere,
            anywhere,
            in_smem,
            in_smem,
            anywhere,
            anywhere,
            anywhere,
        ],
        out_specs=(in_vmem, in_vmem),
        scratch_shapes=[
            pltpu.VMEM((length, features), BF16),
            pltpu.VMEM((features // HEAD_SIZE, HEAD_SIZE), BF16),
            pltpu.VMEM((features, width), BF16),
            pltpu.VMEM((n_set, cached * n_seq, width), BF16),
            pltpu.VMEM((tokens, QUERY_HEADS * HEAD_SIZE), BF16),
            pltpu.VMEM((tokens, 2 * KEY_COLUMNS), BF16),
            pltpu.VMEM(rotary.shape, F32),
            pltpu.VMEM((length, features), BF16),
            pltpu.VMEM((per_set, length, HEAD_SIZE), F32),
            pltpu.VMEM((per_set, length, HEAD_SIZE), BF16),
            pltpu.VMEM((2, per_set, length, HEAD_SIZE), BF16),
            pltpu.VMEM((8, length), F32),
            pltpu.VMEM((2, 8, length), F32),
            pltpu.VMEM((2, length, HEAD_SIZE), F32),
            pltpu.VMEM((blocks, length, HEAD_SIZE), BF16),
            pltpu.VMEM((KEY_HEADS, GROUP * tokens, HEAD_SIZE), BF16),
            pltpu.VMEM((KEY_HEADS, GROUP * tokens, HEAD_SIZE), F32),
            pltpu.VMEM((KEY_HEADS, GROUP * tokens, 2 * HEAD_SIZE), F32),
            dma((halves + 6,)),
            dma((1,)),
            dma((2,)),
            dma((chunks,)),
            dma((2, chunks)),
            dma((2, n_seq)),
            dma((n_seq,)),
            dma((n_x - 1,)),
            dma((n_seq, n_x - 1)),
            dma((n_x,)),
            dma((n_x,)),
            dma((1,)),
            dma((chunks,)),
            dma((n_x - 1,)),
            dma((chunks, n_x - 1)),
            dma((n_x,)),
            dma((per_set, n_x)),
        ],
        compiler_params=pltpu.CompilerParams(
            collective_id=0, has_side_effects=True, vmem_limit_bytes=40 << 20
        ),
        name="project_gather_attend",
    )(
        far(span_hidden),
        far(gain),
        far(key_value_weight),
        far(prompt_key_value),
        span_offset,
        cont_lengths,
        far(cont_query),
        far(continuation_key_value),
        far(rotary),
    )
    return pl.pallas_call(
        hand_on,
        out_shape=(
            jax.ShapeDtypeStruct((rows, width), BF16),
            jax.ShapeDtypeStruct((1, tokens, QUERY_HEADS * HEAD_SIZE), BF16),
        ),
        in_specs=[anywhere, anywhere],
        out_specs=(anywhere, anywhere),
        scratch_shapes=[dma((2,))],
        compiler_params=pltpu.CompilerParams(vmem_limit_bytes=1 << 20),
        name="hand_on",
    )(span_rows, attended)


def solution(mesh):
    placed = (
        P("parts", "seq"),
        P("seq"),
        P("seq", "set"),
        P(("parts", "seq"), None),
        P("parts"),
        P(("parts", "set", "seq"), None, None),
        P(("parts", "set", "seq"), None, None),
        P(("parts", "set", "seq")),
    )
    return jax.shard_map(
        functools.partial(on_device, mesh.shape["set"], mesh.shape["seq"]),
        mesh=mesh,
        in_specs=placed,
        out_specs=(P(("parts", "seq"), "set"), P(("parts", "set", "seq"), None, None)),
        check_vma=False,
    )
```

```python
import functools
import math

import jax
import jax.numpy as jnp
import numpy as np
from jax import lax
from jax.experimental import pallas as pl
from jax.experimental.pallas import tpu as pltpu
from jax.sharding import PartitionSpec as P

MODEL_WIDTH = 8192
QUERY_HEADS = 64
KEY_HEADS = 8
HEAD_SIZE = 128
GROUP = QUERY_HEADS // KEY_HEADS
KEY_COLUMNS = KEY_HEADS * HEAD_SIZE

EPS = 1e-05
NEGATIVE_LARGE = -1e30
EXPONENT = HEAD_SIZE ** (-0.5) * math.log2(math.e)

MESH = pl.DeviceIdType.MESH
HOP, PACE, TWIN_HOP = 3.0, 0.65, 1.4
PASS = {"not_end": (2.85, 4.5, 6.3), "end": (5.0, 5.1, 7.5)}
CROSS = {"not_end": (9.0, 9.1, 10.4), "end": (8.05, 8.15, 11.0)}
WINDOW, LEAD = 4, 7.9
SPLIT, FREE = 0, 3
F32 = jnp.float32
BF16 = jnp.bfloat16


def frequencies():
    index = np.arange(HEAD_SIZE // 2, dtype=np.float64)
    base = 500000.0 ** (-2.0 * index / HEAD_SIZE)
    wave = 2.0 * np.pi / base
    smooth = (8192.0 / wave - 1.0) / 3.0
    blended = (1.0 - smooth) * base / 8.0 + smooth * base
    table = np.where(wave < 2048.0, base, np.where(wave > 8192.0, base / 8.0, blended))
    return np.concatenate([table, table])


def rotary_constants(rows):
    frequency = frequencies()
    sign = np.where(np.arange(HEAD_SIZE) < HEAD_SIZE // 2, -1.0, 1.0)
    angles = np.arange(rows, dtype=np.float64)[:, None] * frequency
    ends = np.ones((8, HEAD_SIZE))
    cosine = np.concatenate([np.cos(angles), ends * frequency])
    sine = np.concatenate([sign * np.sin(angles), ends * sign])
    return np.stack([cosine, sine]).astype(np.float32)


def turn(value, cosine, sine):
    return value * cosine + pltpu.roll(value, HEAD_SIZE // 2, 1) * sine


def scores_of(query, keys):
    return lax.dot_general(query, keys, (((1,), (1,)), ((), ())), preferred_element_type=F32)


def with_ones(values):
    return jnp.concatenate([values, jnp.ones_like(values)], axis=1)


def kernel(
    n_set,
    n_seq,
    pieces,
    hidden_hbm,
    gain_hbm,
    weight_hbm,
    prompt_hbm,
    offset_smem,
    length_smem,
    query_hbm,
    own_hbm,
    rotary_hbm,
    span_out,
    attended_out,
    hidden,
    gain,
    weight,
    prompt,
    query_in,
    own,
    rotary,
    scaled,
    partial,
    sending,
    arriving,
    square_sum,
    square_theirs,
    turns,
    span,
    query,
    best,
    accum,
    load_sem,
    square_send,
    square_recv,
    sum_send,
    sum_recv,
    pz_send,
    pz_recv,
    px_send,
    px_recv,
    pc_send,
    pc_recv,
    sz_send,
    sz_recv,
    sx_send,
    sx_recv,
    sc_send,
    sc_recv,
):
    n_x = n_set // 2
    me_set = lax.axis_index("set")
    me_seq = lax.axis_index("seq")
    me_x, me_core = me_set // 2, me_set % 2
    length, features = hidden.shape
    width = weight.shape[1]
    rows = length // n_seq
    cached = prompt.shape[1] // n_seq
    tokens = query_in.shape[0]
    halves = 2 if width % 512 == 0 else 1
    half = width // halves
    per_set = width // HEAD_SIZE
    per_half = per_set // halves
    part = length // pieces
    chunks = [(j, r) for j in range(per_set) for r in range(pieces)]

    middle = n_seq // 2
    lower = me_seq < middle
    inward = jnp.where(lower, 1, -1)
    inner, outer = me_seq + inward, me_seq - inward
    is_end = jnp.logical_or(me_seq == 0, me_seq == n_seq - 1)
    not_end = jnp.logical_not(is_end)
    is_middle = jnp.logical_or(me_seq == middle - 1, me_seq == middle)
    not_middle = jnp.logical_not(is_middle)
    slot = jnp.where(is_middle, 1, 0)
    has_low, has_high = me_seq > 0, me_seq < n_seq - 1
    twin = me_x * 2 + 1 - me_core

    def set_at(step):
        return ((me_x + step) % n_x) * 2 + me_core

    def twin_at(step):
        return ((me_x + step) % n_x) * 2 + 1 - me_core

    def rows_of(which, count):
        return pl.ds(pl.multiple_of(which * count, count), count)

    loads = []

    def load(source, target):
        copy = pltpu.make_async_copy(source, target, load_sem.at[len(loads)])
        copy.start()
        loads.append(copy)
        return copy

    hidden_load = load(hidden_hbm, hidden)
    gain_load = load(gain_hbm, gain)
    prompt_sem = load_sem.at[len(loads)]
    for s in range(n_set):
        pltpu.make_async_copy(
            prompt_hbm.at[:, pl.ds(s * width, width)],
            prompt.at[s, rows_of(me_seq, cached), :],
            prompt_sem,
        ).start()
    landed = prompt.at[:, rows_of(me_seq, cached), :]
    loads.append(pltpu.make_async_copy(landed, landed, prompt_sem))
    prompt_loads = [loads[-1]]

    def load_weight(i):
        columns = pl.ds(i * half, half)
        return load(weight_hbm.at[:, columns], weight.at[:, columns])

    weight_loads = [load_weight(0)]

    barrier = pltpu.get_barrier_semaphore()

    def greet(device):
        pl.semaphore_signal(barrier, inc=1, device_id=device, device_id_type=MESH)

    others = range(n_seq - 1)

    def other_seq(j):
        upper = (2 * me_seq) // n_seq
        low = j + (j - me_seq + n_seq) // n_seq
        down = n_seq - 1 - j
        high = down - (me_seq - down + n_seq) // n_seq
        return low + upper * (high - low)

    def ends_at(z):
        return jnp.logical_or(z == 0, z == n_seq - 1)

    for e in range(1, n_x):
        greet({"set": set_at(e)})
    greet({"set": twin})
    for j in others:
        z = other_seq(j)
        sends_here = jnp.logical_or(jnp.logical_not(ends_at(z)), jnp.abs(z - me_seq) == 1)

        @pl.when(sends_here)
        def _(z=z):
            greet({"seq": z})

    waits = []

    def remote(source, target, send_sem, recv_sem, device):
        return pltpu.make_async_remote_copy(
            src_ref=source,
            dst_ref=target,
            send_sem=send_sem,
            recv_sem=recv_sem,
            device_id=device,
            device_id_type=MESH,
        )

    def book(make, when=None):
        waits.append((make, when))

    def start(makes):
        for make in makes:
            make().start()

    def prompt_block(s, z):
        return prompt.at[s, rows_of(z, cached), :]

    def span_block(s, c):
        j, r = chunks[c]
        return span.at[s * per_set + j, pl.ds(r * part, part), :]

    def chunk_of(ref, c):
        j, r = chunks[c]
        return ref.at[j, pl.ds(r * part, part), :]

    def project(i):
        columns = pl.ds(i * half, half)
        product = jnp.dot(scaled[...], weight[:, columns], preferred_element_type=F32)
        for j in range(per_half):
            partial[i * per_half + j] = product[:, j * HEAD_SIZE : (j + 1) * HEAD_SIZE]

    def sum_of(c):
        return lambda: remote(
            chunk_of(sending, c),
            chunk_of(arriving.at[slot], c),
            sum_send.at[c],
            sum_recv.at[slot, c],
            {"seq": inner},
        )

    def square_of():
        return remote(
            square_sum,
            square_theirs.at[slot],
            square_send.at[0],
            square_recv.at[slot],
            {"seq": inner},
        )

    sums = [sum_of(c) for c in range(len(chunks))]
    for c in range(len(chunks)):
        book(sums[c], is_end if c + WINDOW < len(chunks) else None)
    square_copies = [square_of]
    book(square_of)

    def reduce_start(c):
        chunk_of(sending, c)[...] = chunk_of(partial, c)[...].astype(BF16)

    def reduce_more(c):
        come = chunk_of(arriving.at[0], c)
        remote(come, come, sum_send.at[c], sum_recv.at[0, c], {"seq": inner}).wait_recv()
        value = chunk_of(partial, c)[...] + come[...].astype(F32)
        chunk_of(partial, c)[...] = value
        chunk_of(sending, c)[...] = value.astype(BF16)

    def square_more():
        come = square_theirs.at[0]
        remote(come, come, square_send.at[0], square_recv.at[0], {"seq": inner}).wait_recv()
        square_sum[...] += come[...]

    def square_last():
        come = square_theirs.at[1]
        remote(come, come, square_send.at[0], square_recv.at[1], {"seq": inner}).wait_recv()
        total = square_sum[...] + come[...]
        column = jnp.broadcast_to(total[0:1, :], (HEAD_SIZE, length)).T
        inverse = lax.rsqrt(column / MODEL_WIDTH + EPS)
        is_key = me_set * width < KEY_COLUMNS
        cosine, sine = angles_at(0, length)
        turns[0] = jnp.where(is_key, cosine, 1.0) * inverse
        turns[1] = jnp.where(is_key, sine, 0.0) * inverse

    def angles_at(first, count):
        base = rotary.shape[1] - 8
        sign = rotary[1, base : base + 1, :]
        moved = rotary[0, base : base + 1, :] * offset_smem[0].astype(F32)
        cos_moved, sin_moved = jnp.cos(moved), jnp.sin(moved) * sign
        cosine, sine = rotary[0, first : first + count, :], rotary[1, first : first + count, :]
        return (
            cosine * cos_moved - sine * sin_moved,
            sine * cos_moved + cosine * sin_moved,
        )

    def finish(c):
        come = chunk_of(arriving.at[1], c)
        remote(come, come, sum_send.at[c], sum_recv.at[1, c], {"seq": inner}).wait_recv()
        block = chunk_of(partial, c)[...] + come[...].astype(F32)
        r = chunks[c][1]
        cosine, sine = (turns[k, pl.ds(r * part, part), :] for k in range(2))
        span_block(me_set, c)[...] = turn(block, cosine, sine).astype(BF16)

    def receive(c):
        mine = span_block(me_set, c)
        remote(mine, mine, sz_send.at[0], sz_recv.at[c], {"seq": outer}).wait_recv()

    def outward_of(c):
        mine = span_block(me_set, c)
        return lambda: remote(mine, mine, sz_send.at[0], sz_recv.at[c], {"seq": outer})

    def across_of(c, e):
        mine = span_block(me_set, c)
        return lambda: remote(
            mine, mine, sx_send.at[e - 1], sx_recv.at[c, e - 1], {"set": set_at(e)}
        )

    def twin_of(c, e):
        block = span_block(set_at(n_x - e), c)
        return lambda: remote(block, block, sc_send.at[e], sc_recv.at[chunks[c][0], e], {"set": twin})

    def count(make):
        return [make(c) for c in range(len(chunks))]

    def span_set(s):
        return span.at[pl.ds(s * per_set, per_set)]

    outward = count(outward_of)
    across = [count(functools.partial(across_of, e=e)) for e in range(1, n_x)]
    twins = [count(functools.partial(twin_of, e=e)) for e in range(n_x)]
    whole = span_set(me_set)
    book(lambda: remote(whole, whole, sz_send.at[0], sz_recv.at[0], {"seq": outer}), not_end)
    for e in range(1, n_x):
        book(
            functools.partial(
                remote, whole, whole, sx_send.at[e - 1], sx_recv.at[0, e - 1], {"set": twin}
            )
        )
    for e in range(n_x):
        came = span_set(set_at(n_x - e))
        book(
            functools.partial(remote, came, came, sc_send.at[e], sc_recv.at[0, e], {"set": twin})
        )

    def spread(c):
        for copies in across:
            copies[c]().start()
        twins[0][c]().start()

    def cross(c):
        for e in range(1, n_x):
            come = span_block(set_at(n_x - e), c)
            remote(come, come, sx_send.at[e - 1], sx_recv.at[c, e - 1], {"set": twin}).wait_recv()
            twins[e][c]().start()

    def crossed(j):
        for e in range(n_x):
            come = span.at[twin_at(n_x - e) * per_set + j]
            remote(come, come, sc_send.at[e], sc_recv.at[j, e], {"set": twin}).wait_recv()

    relays = jnp.logical_and(not_end, ends_at(outer))

    def prompt_to(source, z, which):
        block = prompt_block(me_set, source)
        return lambda: remote(
            block, block, pz_send.at[which, z], pz_recv.at[source], {"seq": z}
        )

    def prompt_across(z, e):
        block = prompt_block(me_set, z)
        return lambda: remote(
            block, block, px_send.at[e - 1], px_recv.at[z, e - 1], {"set": set_at(e)}
        )

    def prompt_twin(z, e):
        block = prompt_block(set_at(n_x - e), z)
        return lambda: remote(block, block, pc_send.at[e], pc_recv.at[e], {"set": twin})

    own_prompt, far_prompt = [], []
    for j in others:
        z = other_seq(j)
        reached = jnp.logical_or(not_end, z == inner)
        own_prompt.append((prompt_to(me_seq, z, 0), reached))
        passed = jnp.logical_and(relays, z != outer)
        far_prompt.append((prompt_to(outer, z, 1), passed))
        book(*own_prompt[-1])
        book(*far_prompt[-1])

    def all_blocks(s):
        return prompt.at[s, pl.ds(0, (n_seq - 1) * cached), :]

    sent = all_blocks(me_set)
    for e in range(1, n_x):
        book(
            functools.partial(
                remote, sent, sent, px_send.at[e - 1], px_recv.at[0, e - 1], {"set": twin}
            )
        )
    for e in range(n_x):
        book(functools.partial(remote, sent, sent, pc_send.at[e], pc_recv.at[e], {"set": twin}))

    def send_prompt():
        for make, when in reversed(own_prompt):
            pl.when(when)(lambda make=make: make().start())

    def pass_prompt(j):
        z = other_seq(j)
        block = prompt_block(me_set, z)
        remote(block, block, pz_send.at[0, z], pz_recv.at[z], {"seq": z}).wait_recv()

        @pl.when(jnp.logical_and(relays, z == outer))
        def _():
            for make, when in far_prompt:
                pl.when(when)(lambda make=make: make().start())

        for e in range(1, n_x):
            prompt_across(z, e)().start()
        prompt_twin(z, 0)().start()

    def cross_prompt(j):
        z = other_seq(j)
        for e in range(1, n_x):
            come = prompt_block(set_at(n_x - e), z)
            remote(
                come, come, px_send.at[e - 1], px_recv.at[z, e - 1], {"set": twin}
            ).wait_recv()
            prompt_twin(z, e)().start()

    def crossed_prompt():
        for e in range(n_x):
            come = all_blocks(twin_at(n_x - e))
            remote(come, come, pc_send.at[e], pc_recv.at[e], {"set": twin}).wait_recv()

    def columns_of(head):
        return pl.ds(head * HEAD_SIZE, HEAD_SIZE)

    causal = jnp.concatenate(
        [
            lax.broadcasted_iota(jnp.int32, (tokens, tokens), 0)
            >= lax.broadcasted_iota(jnp.int32, (tokens, tokens), 1)
        ]
        * GROUP,
        axis=0,
    )
    live = lax.broadcasted_iota(jnp.int32, (1, prompt.shape[1]), 1) < offset_smem[0]
    kept = lax.broadcasted_iota(jnp.int32, (tokens, HEAD_SIZE), 0) < length_smem[0]

    def turn_query(head, cosine, sine):
        for g in range(GROUP):
            raw = query_in[:, columns_of(head * GROUP + g)].astype(F32)
            query[head, g * tokens : (g + 1) * tokens, :] = turn(raw, cosine, sine).astype(BF16)

    def attend_own(head, cosine, sine):
        turn_query(head, cosine, sine)
        keys = turn(own[:, columns_of(head)].astype(F32), cosine, sine).astype(BF16)
        values = own[:, columns_of(head + KEY_HEADS)]
        scores = jnp.where(causal, scores_of(query[head], keys), NEGATIVE_LARGE)
        top = jnp.max(scores, axis=1, keepdims=True)
        weights = jnp.exp2((scores - top) * EXPONENT).astype(BF16)
        best[head] = jnp.broadcast_to(top, best.shape[1:])
        accum[head] = jnp.dot(weights, with_ones(values), preferred_element_type=F32)

    def prompt_head(head):
        return prompt[head // per_set, :, columns_of(head % per_set)]

    def attend_more(head, sources):
        parts = []
        for keys, values, mask in sources:
            scores = scores_of(query[head], keys)
            if mask is not None:
                scores = jnp.where(mask, scores, NEGATIVE_LARGE)
            parts.append((scores, values))
        old = best[head]
        top = old
        for scores, _ in parts:
            top = jnp.maximum(top, jnp.max(scores, axis=1, keepdims=True))
        total = accum[head] * jnp.concatenate([jnp.exp2((old - top) * EXPONENT)] * 2, axis=1)
        for scores, values in parts:
            spread_top = jnp.concatenate([top] * (scores.shape[1] // HEAD_SIZE), axis=1)
            weights = jnp.exp2((scores - spread_top) * EXPONENT).astype(BF16)
            total += jnp.dot(weights, with_ones(values), preferred_element_type=F32)
        return top, total

    def prompt_source(head):
        return prompt_head(head), prompt_head(head + KEY_HEADS), live

    def attend_prompt(head):
        top, total = attend_more(head, [prompt_source(head)])
        best[head] = top
        accum[head] = total

    def attend_last(head, with_prompt):
        sources = [(span[head], span[head + KEY_HEADS], None)]
        if with_prompt:
            sources = [prompt_source(head)] + sources
        _, total = attend_more(head, sources)
        mixed = total[:, :HEAD_SIZE] / total[:, HEAD_SIZE:]
        for g in range(GROUP):
            column = (head * GROUP + g) * HEAD_SIZE
            attended_out[:, column : column + HEAD_SIZE] = jnp.where(
                kept, mixed[g * tokens : (g + 1) * tokens, :], 0.0
            ).astype(BF16)

    hidden_load.wait()
    gain_load.wait()
    squares = jnp.zeros((length, HEAD_SIZE), F32)
    for i in range(features // HEAD_SIZE):
        block = hidden[:, i * HEAD_SIZE : (i + 1) * HEAD_SIZE]
        wide = block.astype(F32)
        squares += wide * wide
        scaled[:, i * HEAD_SIZE : (i + 1) * HEAD_SIZE] = block * gain[i : i + 1, :]
    turns[0] = squares
    for copy in prompt_loads:
        copy.wait()
    weight_loads.extend(load_weight(i) for i in range(1, halves))
    rotary_load = load(rotary_hbm, rotary)
    own_load = load(own_hbm.at[0], own)
    query_load = load(query_hbm.at[0], query_in)
    def meet():
        lines = jnp.where(is_end, 1, n_seq - 1)
        pl.semaphore_wait(barrier, n_x + lines)
        send_prompt()

    pl.when(is_end)(meet)
    weight_loads[0].wait()
    project(0)

    hop, pace, twin_hop = HOP, PACE, TWIN_HOP
    n_chunks = len(chunks)
    final = hop + pace * LEAD
    agenda = []

    def at(time, do, who=None):
        agenda.append((time, len(agenda), who, do))

    def start_sum(c):
        reduce_start(c)
        sums[c]().start()

    def project_rest():
        for i in range(1, halves):
            weight_loads[i].wait()
            project(i)

    def sum_squares():
        square_row = jnp.sum(turns[0].T, axis=0, keepdims=True)
        square_sum[...] = jnp.broadcast_to(square_row, square_sum.shape)

    def more_sum(c):
        reduce_more(c)
        if c >= WINDOW:
            sums[c - WINDOW]().wait_send()
        sums[c]().start()

    def more_square():
        square_more()
        start(square_copies)

    def finish_one(c):
        finish(c)
        pl.when(not_end)(lambda: outward[c]().start())
        spread(c)

    def receive_one(c):
        receive(c)
        pl.when(not_end)(lambda: outward[c]().start())
        spread(c)

    def ready_for_own():
        rotary_load.wait()
        own_load.wait()
        query_load.wait()

    def own_heads(heads):
        own_cosine, own_sine = angles_at(length, tokens)
        for head in heads:
            attend_own(head, own_cosine, own_sine)

    def store_span():
        for j in range(per_set):
            span_out[:, columns_of(j)] = span[me_set * per_set + j, rows_of(me_seq, rows), :]

    own_time, project_time = 0.33, 0.8
    at(project_time + 0.05, meet, "not_end")
    at(0.1, sum_squares)
    at(0.15, lambda: start(square_copies), "end")
    at(0.2, project_rest)
    for c in range(n_chunks):
        when = 0.05 * c if c < per_half * pieces // 2 else project_time + pace * (c - 2)
        at(when, functools.partial(start_sum, c), "end")
    at(project_time, ready_for_own)
    for head in range(0, KEY_HEADS, 2):
        heads = range(head, head + 2)
        at(project_time + own_time * (head + 0.5), functools.partial(own_heads, heads))
    for c in range(n_chunks):
        at(hop + pace * c, functools.partial(more_sum, c), "not_end")
        at(final + pace * c + 0.005, functools.partial(finish_one, c), "middle")
        at(final + hop + pace * c, functools.partial(cross, c), "middle")
        at(final + hop + pace * c, functools.partial(receive_one, c), "not_middle")
        at(final + 2 * hop + pace * c, functools.partial(cross, c), "not_middle")
    at(hop + 0.01, more_square, "not_end")
    at(final, square_last, "middle")

    for j in others:
        step = min(2, j * 3 // (n_seq - 1))
        for who in ("not_end", "end"):
            at(PASS[who][step], functools.partial(pass_prompt, j), who)
            at(CROSS[who][step], functools.partial(cross_prompt, j), who)

    def prompt_heads(heads):
        for head in heads:
            attend_prompt(head)

    groups = [[h for h in range(KEY_HEADS) if h % per_set == j] for j in range(per_set)]
    split = min(SPLIT, per_set)
    free = final + hop + pace * FREE + 0.02
    at(free, crossed_prompt)
    for k in range(split, per_set):
        at(free + 0.01 + pace * (k - split), functools.partial(prompt_heads, groups[k]))
    for j in range(per_set):
        arrived = final + 2 * hop + pace * ((j + 1) * pieces - 1) + twin_hop
        if j + 1 == per_set:
            at(arrived - 0.5, store_span)

        def last_heads(j=j):
            crossed(j)
            for head in groups[j]:
                attend_last(head, j < split)

        at(arrived, last_heads)

    who_is = {
        "end": is_end,
        "not_end": not_end,
        "middle": is_middle,
        "not_middle": not_middle,
    }
    agenda.sort(key=lambda entry: entry[:2])
    while agenda:
        time, _, who, _ = agenda[0]
        group = []
        while agenda and agenda[0][2] == who and (who is not None or not group):
            group.append(agenda.pop(0)[3])

        def run(group=group):
            for do in group:
                do()

        if who is None:
            run()
        else:
            pl.when(who_is[who])(run)

    for make, when in waits:
        if when is None:
            make().wait_send()
        else:
            pl.when(when)(lambda make=make: make().wait_send())


def hand_on(span_in, attended_in, span_out, attended_out, sem):
    copies = [
        pltpu.make_async_copy(attended_in, attended_out.at[0], sem.at[0]),
        pltpu.make_async_copy(span_in, span_out, sem.at[1]),
    ]
    for copy in copies:
        copy.start()
    for copy in copies:
        copy.wait()


def on_device(
    n_set,
    n_seq,
    span_hidden,
    norm_gain,
    key_value_weight,
    prompt_key_value,
    span_offset,
    cont_query,
    continuation_key_value,
    cont_lengths,
):
    length, features = span_hidden.shape
    width = key_value_weight.shape[1]
    rows = length // n_seq
    cached = prompt_key_value.shape[0]
    tokens = cont_query.shape[1]
    n_x = n_set // 2
    halves = 2 if width % 512 == 0 else 1
    pieces = 2
    per_set = width // HEAD_SIZE
    blocks = n_set * per_set
    chunks = per_set * pieces
    rotary = jnp.asarray(rotary_constants(length + tokens))
    gain = norm_gain.reshape(features // HEAD_SIZE, HEAD_SIZE)
    dma = pltpu.SemaphoreType.DMA
    anywhere = pl.BlockSpec(memory_space=pl.ANY)
    in_vmem = pl.BlockSpec(memory_space=pltpu.VMEM)
    in_smem = pl.BlockSpec(memory_space=pltpu.SMEM)

    def far(array):
        return pltpu.with_memory_space_constraint(array, pltpu.HBM)

    span_rows, attended = pl.pallas_call(
        functools.partial(kernel, n_set, n_seq, pieces),
        out_shape=(
            pltpu.VMEM((rows, width), BF16),
            pltpu.VMEM((tokens, QUERY_HEADS * HEAD_SIZE), BF16),
        ),
        in_specs=[
            anywhere,
            anywhere,
            anywhere,
            anywhere,
            in_smem,
            in_smem,
            anywhere,
            anywhere,
            anywhere,
        ],
        out_specs=(in_vmem, in_vmem),
        scratch_shapes=[
            pltpu.VMEM((length, features), BF16),
            pltpu.VMEM((features // HEAD_SIZE, HEAD_SIZE), BF16),
            pltpu.VMEM((features, width), BF16),
            pltpu.VMEM((n_set, cached * n_seq, width), BF16),
            pltpu.VMEM((tokens, QUERY_HEADS * HEAD_SIZE), BF16),
            pltpu.VMEM((tokens, 2 * KEY_COLUMNS), BF16),
            pltpu.VMEM(rotary.shape, F32),
            pltpu.VMEM((length, features), BF16),
            pltpu.VMEM((per_set, length, HEAD_SIZE), F32),
            pltpu.VMEM((per_set, length, HEAD_SIZE), BF16),
            pltpu.VMEM((2, per_set, length, HEAD_SIZE), BF16),
            pltpu.VMEM((8, length), F32),
            pltpu.VMEM((2, 8, length), F32),
            pltpu.VMEM((2, length, HEAD_SIZE), F32),
            pltpu.VMEM((blocks, length, HEAD_SIZE), BF16),
            pltpu.VMEM((KEY_HEADS, GROUP * tokens, HEAD_SIZE), BF16),
            pltpu.VMEM((KEY_HEADS, GROUP * tokens, HEAD_SIZE), F32),
            pltpu.VMEM((KEY_HEADS, GROUP * tokens, 2 * HEAD_SIZE), F32),
            dma((halves + 6,)),
            dma((1,)),
            dma((2,)),
            dma((chunks,)),
            dma((2, chunks)),
            dma((2, n_seq)),
            dma((n_seq,)),
            dma((n_x - 1,)),
            dma((n_seq, n_x - 1)),
            dma((n_x,)),
            dma((n_x,)),
            dma((1,)),
            dma((chunks,)),
            dma((n_x - 1,)),
            dma((chunks, n_x - 1)),
            dma((n_x,)),
            dma((per_set, n_x)),
        ],
        compiler_params=pltpu.CompilerParams(
            collective_id=0, has_side_effects=True, vmem_limit_bytes=40 << 20
        ),
        name="project_gather_attend",
    )(
        far(span_hidden),
        far(gain),
        far(key_value_weight),
        far(prompt_key_value),
        span_offset,
        cont_lengths,
        far(cont_query),
        far(continuation_key_value),
        far(rotary),
    )
    return pl.pallas_call(
        hand_on,
        out_shape=(
            jax.ShapeDtypeStruct((rows, width), BF16),
            jax.ShapeDtypeStruct((1, tokens, QUERY_HEADS * HEAD_SIZE), BF16),
        ),
        in_specs=[anywhere, anywhere],
        out_specs=(anywhere, anywhere),
        scratch_shapes=[dma((2,))],
        compiler_params=pltpu.CompilerParams(vmem_limit_bytes=1 << 20),
        name="hand_on",
    )(span_rows, attended)


def solution(mesh):
    placed = (
        P("parts", "seq"),
        P("seq"),
        P("seq", "set"),
        P(("parts", "seq"), None),
        P("parts"),
        P(("parts", "set", "seq"), None, None),
        P(("parts", "set", "seq"), None, None),
        P(("parts", "set", "seq")),
    )
    return jax.shard_map(
        functools.partial(on_device, mesh.shape["set"], mesh.shape["seq"]),
        mesh=mesh,
        in_specs=placed,
        out_specs=(P(("parts", "seq"), "set"), P(("parts", "set", "seq"), None, None)),
        check_vma=False,
    )
```

```python
import functools
import math

import jax
import jax.numpy as jnp
import numpy as np
from jax import lax
from jax.experimental import pallas as pl
from jax.experimental.pallas import tpu as pltpu
from jax.sharding import PartitionSpec as P

MODEL_WIDTH = 8192
QUERY_HEADS = 64
KEY_HEADS = 8
HEAD_SIZE = 128
GROUP = QUERY_HEADS // KEY_HEADS
KEY_COLUMNS = KEY_HEADS * HEAD_SIZE

EPS = 1e-05
NEGATIVE_LARGE = -1e30
EXPONENT = HEAD_SIZE ** (-0.5) * math.log2(math.e)

MESH = pl.DeviceIdType.MESH
HOP, PACE, TWIN_HOP = 3.0, 0.65, 1.4
PASS = {"not_end": (2.85, 4.5, 6.3), "end": (5.0, 5.1, 7.5)}
CROSS = {"not_end": (9.0, 9.1, 10.4), "end": (8.05, 8.15, 11.0)}
LEAD = 7.9
SPLIT, FREE = 0, 2
F32 = jnp.float32
BF16 = jnp.bfloat16


def frequencies():
    index = np.arange(HEAD_SIZE // 2, dtype=np.float64)
    base = 500000.0 ** (-2.0 * index / HEAD_SIZE)
    wave = 2.0 * np.pi / base
    smooth = (8192.0 / wave - 1.0) / 3.0
    blended = (1.0 - smooth) * base / 8.0 + smooth * base
    table = np.where(wave < 2048.0, base, np.where(wave > 8192.0, base / 8.0, blended))
    return np.concatenate([table, table])


def rotary_constants(rows):
    frequency = frequencies()
    sign = np.where(np.arange(HEAD_SIZE) < HEAD_SIZE // 2, -1.0, 1.0)
    angles = np.arange(rows, dtype=np.float64)[:, None] * frequency
    ends = np.ones((8, HEAD_SIZE))
    cosine = np.concatenate([np.cos(angles), ends * frequency])
    sine = np.concatenate([sign * np.sin(angles), ends * sign])
    return np.stack([cosine, sine]).astype(np.float32)


def turn(value, cosine, sine):
    return value * cosine + pltpu.roll(value, HEAD_SIZE // 2, 1) * sine


def scores_of(query, keys):
    return lax.dot_general(query, keys, (((1,), (1,)), ((), ())), preferred_element_type=F32)


def with_ones(values):
    return jnp.concatenate([values, jnp.ones_like(values)], axis=1)


def kernel(
    n_set,
    n_seq,
    pieces,
    hidden_hbm,
    gain_hbm,
    weight_hbm,
    prompt_hbm,
    offset_smem,
    length_smem,
    query_hbm,
    own_hbm,
    rotary_hbm,
    span_out,
    attended_out,
    hidden,
    gain,
    weight,
    prompt,
    query_in,
    own,
    rotary,
    scaled,
    partial,
    sending,
    arriving,
    square_sum,
    square_theirs,
    turns,
    span,
    query,
    best,
    accum,
    load_sem,
    square_send,
    square_recv,
    sum_send,
    sum_recv,
    pz_send,
    pz_recv,
    px_send,
    px_recv,
    pc_send,
    pc_recv,
    sz_send,
    sz_recv,
    sx_send,
    sx_recv,
    sc_send,
    sc_recv,
):
    n_x = n_set // 2
    me_set = lax.axis_index("set")
    me_seq = lax.axis_index("seq")
    me_x, me_core = me_set // 2, me_set % 2
    length, features = hidden.shape
    width = weight.shape[1]
    rows = length // n_seq
    cached = prompt.shape[1] // n_seq
    tokens = query_in.shape[0]
    halves = 2 if width % 512 == 0 else 1
    half = width // halves
    per_set = width // HEAD_SIZE
    per_half = per_set // halves
    part = length // pieces
    chunks = [(j, r) for j in range(per_set) for r in range(pieces)]

    middle = n_seq // 2
    lower = me_seq < middle
    inward = jnp.where(lower, 1, -1)
    inner, outer = me_seq + inward, me_seq - inward
    is_end = jnp.logical_or(me_seq == 0, me_seq == n_seq - 1)
    not_end = jnp.logical_not(is_end)
    is_middle = jnp.logical_or(me_seq == middle - 1, me_seq == middle)
    not_middle = jnp.logical_not(is_middle)
    slot = jnp.where(is_middle, 1, 0)
    has_low, has_high = me_seq > 0, me_seq < n_seq - 1
    twin = me_x * 2 + 1 - me_core

    def set_at(step):
        return ((me_x + step) % n_x) * 2 + me_core

    def twin_at(step):
        return ((me_x + step) % n_x) * 2 + 1 - me_core

    def rows_of(which, count):
        return pl.ds(pl.multiple_of(which * count, count), count)

    loads = []

    def load(source, target):
        copy = pltpu.make_async_copy(source, target, load_sem.at[len(loads)])
        copy.start()
        loads.append(copy)
        return copy

    hidden_load = load(hidden_hbm, hidden)
    gain_load = load(gain_hbm, gain)
    prompt_sem = load_sem.at[len(loads)]
    for s in range(n_set):
        pltpu.make_async_copy(
            prompt_hbm.at[:, pl.ds(s * width, width)],
            prompt.at[s, rows_of(me_seq, cached), :],
            prompt_sem,
        ).start()
    landed = prompt.at[:, rows_of(me_seq, cached), :]
    loads.append(pltpu.make_async_copy(landed, landed, prompt_sem))
    prompt_loads = [loads[-1]]

    def load_weight(i):
        columns = pl.ds(i * half, half)
        return load(weight_hbm.at[:, columns], weight.at[:, columns])

    weight_loads = [load_weight(0)]

    barrier = pltpu.get_barrier_semaphore()

    def greet(device):
        pl.semaphore_signal(barrier, inc=1, device_id=device, device_id_type=MESH)

    others = range(n_seq - 1)

    def other_seq(j):
        upper = (2 * me_seq) // n_seq
        low = j + (j - me_seq + n_seq) // n_seq
        down = n_seq - 1 - j
        high = down - (me_seq - down + n_seq) // n_seq
        return low + upper * (high - low)

    def ends_at(z):
        return jnp.logical_or(z == 0, z == n_seq - 1)

    for e in range(1, n_x):
        greet({"set": set_at(e)})
    greet({"set": twin})
    for j in others:
        z = other_seq(j)
        sends_here = jnp.logical_or(jnp.logical_not(ends_at(z)), jnp.abs(z - me_seq) == 1)

        @pl.when(sends_here)
        def _(z=z):
            greet({"seq": z})

    waits = []

    def remote(source, target, send_sem, recv_sem, device):
        return pltpu.make_async_remote_copy(
            src_ref=source,
            dst_ref=target,
            send_sem=send_sem,
            recv_sem=recv_sem,
            device_id=device,
            device_id_type=MESH,
        )

    def book(make, when=None):
        waits.append((make, when))

    def start(makes):
        for make in makes:
            make().start()

    def prompt_block(s, z):
        return prompt.at[s, rows_of(z, cached), :]

    def span_block(s, c):
        j, r = chunks[c]
        return span.at[s * per_set + j, pl.ds(r * part, part), :]

    def chunk_of(ref, c):
        j, r = chunks[c]
        return ref.at[j, pl.ds(r * part, part), :]

    def project(i):
        columns = pl.ds(i * half, half)
        product = jnp.dot(scaled[...], weight[:, columns], preferred_element_type=F32)
        for j in range(per_half):
            partial[i * per_half + j] = product[:, j * HEAD_SIZE : (j + 1) * HEAD_SIZE]

    def sum_of(c):
        return lambda: remote(
            chunk_of(sending, c),
            chunk_of(arriving.at[slot], c),
            sum_send.at[0],
            sum_recv.at[slot, c],
            {"seq": inner},
        )

    def square_of():
        return remote(
            square_sum,
            square_theirs.at[slot],
            square_send.at[0],
            square_recv.at[slot],
            {"seq": inner},
        )

    sums = [sum_of(c) for c in range(len(chunks))]
    book(lambda: remote(sending, sending, sum_send.at[0], sum_recv.at[0, 0], {"seq": inner}))
    square_copies = [square_of]
    book(square_of)

    def reduce_start(c):
        chunk_of(sending, c)[...] = chunk_of(partial, c)[...].astype(BF16)

    def reduce_more(c):
        come = chunk_of(arriving.at[0], c)
        remote(come, come, sum_send.at[0], sum_recv.at[0, c], {"seq": inner}).wait_recv()
        value = chunk_of(partial, c)[...] + come[...].astype(F32)
        chunk_of(partial, c)[...] = value
        chunk_of(sending, c)[...] = value.astype(BF16)

    def square_more():
        come = square_theirs.at[0]
        remote(come, come, square_send.at[0], square_recv.at[0], {"seq": inner}).wait_recv()
        square_sum[...] += come[...]

    def square_last():
        come = square_theirs.at[1]
        remote(come, come, square_send.at[0], square_recv.at[1], {"seq": inner}).wait_recv()
        total = square_sum[...] + come[...]
        column = jnp.broadcast_to(total[0:1, :], (HEAD_SIZE, length)).T
        inverse = lax.rsqrt(column / MODEL_WIDTH + EPS)
        is_key = me_set * width < KEY_COLUMNS
        cosine, sine = angles_at(0, length)
        turns[0] = jnp.where(is_key, cosine, 1.0) * inverse
        turns[1] = jnp.where(is_key, sine, 0.0) * inverse

    def angles_at(first, count):
        base = rotary.shape[1] - 8
        sign = rotary[1, base : base + 1, :]
        moved = rotary[0, base : base + 1, :] * offset_smem[0].astype(F32)
        cos_moved, sin_moved = jnp.cos(moved), jnp.sin(moved) * sign
        cosine, sine = rotary[0, first : first + count, :], rotary[1, first : first + count, :]
        return (
            cosine * cos_moved - sine * sin_moved,
            sine * cos_moved + cosine * sin_moved,
        )

    def finish(c):
        come = chunk_of(arriving.at[1], c)
        remote(come, come, sum_send.at[0], sum_recv.at[1, c], {"seq": inner}).wait_recv()
        block = chunk_of(partial, c)[...] + come[...].astype(F32)
        r = chunks[c][1]
        cosine, sine = (turns[k, pl.ds(r * part, part), :] for k in range(2))
        span_block(me_set, c)[...] = turn(block, cosine, sine).astype(BF16)

    def receive(c):
        mine = span_block(me_set, c)
        remote(mine, mine, sz_send.at[0], sz_recv.at[c], {"seq": outer}).wait_recv()

    def outward_of(c):
        mine = span_block(me_set, c)
        return lambda: remote(mine, mine, sz_send.at[0], sz_recv.at[c], {"seq": outer})

    def across_of(c, e):
        mine = span_block(me_set, c)
        return lambda: remote(
            mine, mine, sx_send.at[e - 1], sx_recv.at[c, e - 1], {"set": set_at(e)}
        )

    def twin_of(c, e):
        block = span_block(set_at(n_x - e), c)
        return lambda: remote(block, block, sc_send.at[e], sc_recv.at[chunks[c][0], e], {"set": twin})

    def count(make):
        return [make(c) for c in range(len(chunks))]

    def span_set(s):
        return span.at[pl.ds(s * per_set, per_set)]

    outward = count(outward_of)
    across = [count(functools.partial(across_of, e=e)) for e in range(1, n_x)]
    twins = [count(functools.partial(twin_of, e=e)) for e in range(n_x)]
    whole = span_set(me_set)
    book(lambda: remote(whole, whole, sz_send.at[0], sz_recv.at[0], {"seq": outer}), not_end)
    for e in range(1, n_x):
        book(
            functools.partial(
                remote, whole, whole, sx_send.at[e - 1], sx_recv.at[0, e - 1], {"set": twin}
            )
        )
    for e in range(n_x):
        came = span_set(set_at(n_x - e))
        book(
            functools.partial(remote, came, came, sc_send.at[e], sc_recv.at[0, e], {"set": twin})
        )

    def spread(c):
        for copies in across:
            copies[c]().start()
        twins[0][c]().start()

    def cross(c):
        for e in range(1, n_x):
            come = span_block(set_at(n_x - e), c)
            remote(come, come, sx_send.at[e - 1], sx_recv.at[c, e - 1], {"set": twin}).wait_recv()
            twins[e][c]().start()

    def crossed(j):
        for e in range(n_x):
            come = span.at[twin_at(n_x - e) * per_set + j]
            remote(come, come, sc_send.at[e], sc_recv.at[j, e], {"set": twin}).wait_recv()

    relays = jnp.logical_and(not_end, ends_at(outer))

    def prompt_to(source, z, which):
        block = prompt_block(me_set, source)
        return lambda: remote(
            block, block, pz_send.at[which, z], pz_recv.at[source], {"seq": z}
        )

    def prompt_across(z, e):
        block = prompt_block(me_set, z)
        return lambda: remote(
            block, block, px_send.at[e - 1], px_recv.at[z, e - 1], {"set": set_at(e)}
        )

    def prompt_twin(z, e):
        block = prompt_block(set_at(n_x - e), z)
        return lambda: remote(block, block, pc_send.at[e], pc_recv.at[e], {"set": twin})

    own_prompt, far_prompt = [], []
    for j in others:
        z = other_seq(j)
        reached = jnp.logical_or(not_end, z == inner)
        own_prompt.append((prompt_to(me_seq, z, 0), reached))
        passed = jnp.logical_and(relays, z != outer)
        far_prompt.append((prompt_to(outer, z, 1), passed))
        book(*own_prompt[-1])
        book(*far_prompt[-1])

    def all_blocks(s):
        return prompt.at[s, pl.ds(0, (n_seq - 1) * cached), :]

    sent = all_blocks(me_set)
    for e in range(1, n_x):
        book(
            functools.partial(
                remote, sent, sent, px_send.at[e - 1], px_recv.at[0, e - 1], {"set": twin}
            )
        )
    for e in range(n_x):
        book(functools.partial(remote, sent, sent, pc_send.at[e], pc_recv.at[e], {"set": twin}))

    def send_prompt():
        for make, when in reversed(own_prompt):
            pl.when(when)(lambda make=make: make().start())

    def pass_prompt(j):
        z = other_seq(j)
        block = prompt_block(me_set, z)
        remote(block, block, pz_send.at[0, z], pz_recv.at[z], {"seq": z}).wait_recv()

        @pl.when(jnp.logical_and(relays, z == outer))
        def _():
            for make, when in far_prompt:
                pl.when(when)(lambda make=make: make().start())

        for e in range(1, n_x):
            prompt_across(z, e)().start()
        prompt_twin(z, 0)().start()

    def cross_prompt(j):
        z = other_seq(j)
        for e in range(1, n_x):
            come = prompt_block(set_at(n_x - e), z)
            remote(
                come, come, px_send.at[e - 1], px_recv.at[z, e - 1], {"set": twin}
            ).wait_recv()
            prompt_twin(z, e)().start()

    def crossed_prompt():
        for e in range(n_x):
            come = all_blocks(twin_at(n_x - e))
            remote(come, come, pc_send.at[e], pc_recv.at[e], {"set": twin}).wait_recv()

    def columns_of(head):
        return pl.ds(head * HEAD_SIZE, HEAD_SIZE)

    causal = jnp.concatenate(
        [
            lax.broadcasted_iota(jnp.int32, (tokens, tokens), 0)
            >= lax.broadcasted_iota(jnp.int32, (tokens, tokens), 1)
        ]
        * GROUP,
        axis=0,
    )
    live = lax.broadcasted_iota(jnp.int32, (1, prompt.shape[1]), 1) < offset_smem[0]
    kept = lax.broadcasted_iota(jnp.int32, (tokens, HEAD_SIZE), 0) < length_smem[0]

    def turn_query(head, cosine, sine):
        for g in range(GROUP):
            raw = query_in[:, columns_of(head * GROUP + g)].astype(F32)
            query[head, g * tokens : (g + 1) * tokens, :] = turn(raw, cosine, sine).astype(BF16)

    def attend_own(head, cosine, sine):
        turn_query(head, cosine, sine)
        keys = turn(own[:, columns_of(head)].astype(F32), cosine, sine).astype(BF16)
        values = own[:, columns_of(head + KEY_HEADS)]
        scores = jnp.where(causal, scores_of(query[head], keys), NEGATIVE_LARGE)
        top = jnp.max(scores, axis=1, keepdims=True)
        weights = jnp.exp2((scores - top) * EXPONENT).astype(BF16)
        best[head] = jnp.broadcast_to(top, best.shape[1:])
        accum[head] = jnp.dot(weights, with_ones(values), preferred_element_type=F32)

    def prompt_head(head):
        return prompt[head // per_set, :, columns_of(head % per_set)]

    def attend_more(head, sources):
        parts = []
        for keys, values, mask in sources:
            scores = scores_of(query[head], keys)
            if mask is not None:
                scores = jnp.where(mask, scores, NEGATIVE_LARGE)
            parts.append((scores, values))
        old = best[head]
        top = old
        for scores, _ in parts:
            top = jnp.maximum(top, jnp.max(scores, axis=1, keepdims=True))
        total = accum[head] * jnp.concatenate([jnp.exp2((old - top) * EXPONENT)] * 2, axis=1)
        for scores, values in parts:
            spread_top = jnp.concatenate([top] * (scores.shape[1] // HEAD_SIZE), axis=1)
            weights = jnp.exp2((scores - spread_top) * EXPONENT).astype(BF16)
            total += jnp.dot(weights, with_ones(values), preferred_element_type=F32)
        return top, total

    def prompt_source(head):
        return prompt_head(head), prompt_head(head + KEY_HEADS), live

    def attend_prompt(head):
        top, total = attend_more(head, [prompt_source(head)])
        best[head] = top
        accum[head] = total

    def attend_last(head, with_prompt):
        sources = [(span[head], span[head + KEY_HEADS], None)]
        if with_prompt:
            sources = [prompt_source(head)] + sources
        _, total = attend_more(head, sources)
        mixed = total[:, :HEAD_SIZE] / total[:, HEAD_SIZE:]
        for g in range(GROUP):
            column = (head * GROUP + g) * HEAD_SIZE
            attended_out[:, column : column + HEAD_SIZE] = jnp.where(
                kept, mixed[g * tokens : (g + 1) * tokens, :], 0.0
            ).astype(BF16)

    hidden_load.wait()
    gain_load.wait()
    squares = jnp.zeros((length, HEAD_SIZE), F32)
    for i in range(features // HEAD_SIZE):
        block = hidden[:, i * HEAD_SIZE : (i + 1) * HEAD_SIZE]
        wide = block.astype(F32)
        squares += wide * wide
        scaled[:, i * HEAD_SIZE : (i + 1) * HEAD_SIZE] = block * gain[i : i + 1, :]
    turns[0] = squares
    for copy in prompt_loads:
        copy.wait()
    weight_loads.extend(load_weight(i) for i in range(1, halves))
    rotary_load = load(rotary_hbm, rotary)
    own_load = load(own_hbm.at[0], own)
    query_load = load(query_hbm.at[0], query_in)
    def meet():
        lines = jnp.where(is_end, 1, n_seq - 1)
        pl.semaphore_wait(barrier, n_x + lines)
        send_prompt()

    pl.when(is_end)(meet)
    weight_loads[0].wait()
    project(0)

    hop, pace, twin_hop = HOP, PACE, TWIN_HOP
    n_chunks = len(chunks)
    final = hop + pace * LEAD
    agenda = []

    def at(time, do, who=None):
        agenda.append((time, len(agenda), who, do))

    def start_sum(c):
        reduce_start(c)
        sums[c]().start()

    def project_rest():
        for i in range(1, halves):
            weight_loads[i].wait()
            project(i)

    def sum_squares():
        square_row = jnp.sum(turns[0].T, axis=0, keepdims=True)
        square_sum[...] = jnp.broadcast_to(square_row, square_sum.shape)

    def more_sum(c):
        reduce_more(c)
        sums[c]().start()

    def more_square():
        square_more()
        start(square_copies)

    def finish_one(c):
        finish(c)
        pl.when(not_end)(lambda: outward[c]().start())
        spread(c)

    def receive_one(c):
        receive(c)
        pl.when(not_end)(lambda: outward[c]().start())
        spread(c)

    def ready_for_own():
        rotary_load.wait()
        own_load.wait()
        query_load.wait()

    def own_heads(heads):
        own_cosine, own_sine = angles_at(length, tokens)
        for head in heads:
            attend_own(head, own_cosine, own_sine)

    def store_span():
        for j in range(per_set):
            span_out[:, columns_of(j)] = span[me_set * per_set + j, rows_of(me_seq, rows), :]

    own_time, project_time = 0.33, 0.8
    at(project_time + 0.05, meet, "not_end")
    at(0.1, sum_squares)
    at(0.15, lambda: start(square_copies), "end")
    at(0.2, project_rest)
    for c in range(n_chunks):
        when = 0.05 * c if c < per_half * pieces // 2 else project_time + pace * (c - 2)
        at(when, functools.partial(start_sum, c), "end")
    at(project_time, ready_for_own)
    for head in range(0, KEY_HEADS, 2):
        heads = range(head, head + 2)
        at(project_time + own_time * (head + 0.5), functools.partial(own_heads, heads))
    for c in range(n_chunks):
        at(hop + pace * c, functools.partial(more_sum, c), "not_end")
        at(final + pace * c + 0.005, functools.partial(finish_one, c), "middle")
        at(final + hop + pace * c, functools.partial(cross, c), "middle")
        at(final + hop + pace * c, functools.partial(receive_one, c), "not_middle")
        at(final + 2 * hop + pace * c, functools.partial(cross, c), "not_middle")
    at(hop + 0.01, more_square, "not_end")
    at(final, square_last, "middle")

    for j in others:
        step = min(2, j * 3 // (n_seq - 1))
        for who in ("not_end", "end"):
            at(PASS[who][step], functools.partial(pass_prompt, j), who)
            at(CROSS[who][step], functools.partial(cross_prompt, j), who)

    def prompt_heads(heads):
        for head in heads:
            attend_prompt(head)

    groups = [[h for h in range(KEY_HEADS) if h % per_set == j] for j in range(per_set)]
    split = min(SPLIT, per_set)
    free = final + hop + pace * FREE + 0.02
    at(free, crossed_prompt)
    for k in range(split, per_set):
        at(free + 0.01 + pace * (k - split), functools.partial(prompt_heads, groups[k]))
    for j in range(per_set):
        arrived = final + 2 * hop + pace * ((j + 1) * pieces - 1) + twin_hop
        if j + 1 == per_set:
            at(arrived - 0.5, store_span)

        def last_heads(j=j):
            crossed(j)
            for head in groups[j]:
                attend_last(head, j < split)

        at(arrived, last_heads)

    who_is = {
        "end": is_end,
        "not_end": not_end,
        "middle": is_middle,
        "not_middle": not_middle,
    }
    agenda.sort(key=lambda entry: entry[:2])
    while agenda:
        time, _, who, _ = agenda[0]
        group = []
        while agenda and agenda[0][2] == who and (who is not None or not group):
            group.append(agenda.pop(0)[3])

        def run(group=group):
            for do in group:
                do()

        if who is None:
            run()
        else:
            pl.when(who_is[who])(run)

    for make, when in waits:
        if when is None:
            make().wait_send()
        else:
            pl.when(when)(lambda make=make: make().wait_send())


def hand_on(span_in, attended_in, span_out, attended_out, sem):
    copies = [
        pltpu.make_async_copy(attended_in, attended_out.at[0], sem.at[0]),
        pltpu.make_async_copy(span_in, span_out, sem.at[1]),
    ]
    for copy in copies:
        copy.start()
    for copy in copies:
        copy.wait()


def on_device(
    n_set,
    n_seq,
    span_hidden,
    norm_gain,
    key_value_weight,
    prompt_key_value,
    span_offset,
    cont_query,
    continuation_key_value,
    cont_lengths,
):
    length, features = span_hidden.shape
    width = key_value_weight.shape[1]
    rows = length // n_seq
    cached = prompt_key_value.shape[0]
    tokens = cont_query.shape[1]
    n_x = n_set // 2
    halves = 2 if width % 512 == 0 else 1
    pieces = 2
    per_set = width // HEAD_SIZE
    blocks = n_set * per_set
    chunks = per_set * pieces
    rotary = jnp.asarray(rotary_constants(length + tokens))
    gain = norm_gain.reshape(features // HEAD_SIZE, HEAD_SIZE)
    dma = pltpu.SemaphoreType.DMA
    anywhere = pl.BlockSpec(memory_space=pl.ANY)
    in_vmem = pl.BlockSpec(memory_space=pltpu.VMEM)
    in_smem = pl.BlockSpec(memory_space=pltpu.SMEM)

    def far(array):
        return pltpu.with_memory_space_constraint(array, pltpu.HBM)

    span_rows, attended = pl.pallas_call(
        functools.partial(kernel, n_set, n_seq, pieces),
        out_shape=(
            pltpu.VMEM((rows, width), BF16),
            pltpu.VMEM((tokens, QUERY_HEADS * HEAD_SIZE), BF16),
        ),
        in_specs=[
            anywhere,
            anywhere,
            anywhere,
            anywhere,
            in_smem,
            in_smem,
            anywhere,
            anywhere,
            anywhere,
        ],
        out_specs=(in_vmem, in_vmem),
        scratch_shapes=[
            pltpu.VMEM((length, features), BF16),
            pltpu.VMEM((features // HEAD_SIZE, HEAD_SIZE), BF16),
            pltpu.VMEM((features, width), BF16),
            pltpu.VMEM((n_set, cached * n_seq, width), BF16),
            pltpu.VMEM((tokens, QUERY_HEADS * HEAD_SIZE), BF16),
            pltpu.VMEM((tokens, 2 * KEY_COLUMNS), BF16),
            pltpu.VMEM(rotary.shape, F32),
            pltpu.VMEM((length, features), BF16),
            pltpu.VMEM((per_set, length, HEAD_SIZE), F32),
            pltpu.VMEM((per_set, length, HEAD_SIZE), BF16),
            pltpu.VMEM((2, per_set, length, HEAD_SIZE), BF16),
            pltpu.VMEM((8, length), F32),
            pltpu.VMEM((2, 8, length), F32),
            pltpu.VMEM((2, length, HEAD_SIZE), F32),
            pltpu.VMEM((blocks, length, HEAD_SIZE), BF16),
            pltpu.VMEM((KEY_HEADS, GROUP * tokens, HEAD_SIZE), BF16),
            pltpu.VMEM((KEY_HEADS, GROUP * tokens, HEAD_SIZE), F32),
            pltpu.VMEM((KEY_HEADS, GROUP * tokens, 2 * HEAD_SIZE), F32),
            dma((halves + 6,)),
            dma((1,)),
            dma((2,)),
            dma((1,)),
            dma((2, chunks)),
            dma((2, n_seq)),
            dma((n_seq,)),
            dma((n_x - 1,)),
            dma((n_seq, n_x - 1)),
            dma((n_x,)),
            dma((n_x,)),
            dma((1,)),
            dma((chunks,)),
            dma((n_x - 1,)),
            dma((chunks, n_x - 1)),
            dma((n_x,)),
            dma((per_set, n_x)),
        ],
        compiler_params=pltpu.CompilerParams(
            collective_id=0, has_side_effects=True, vmem_limit_bytes=40 << 20
        ),
        name="project_gather_attend",
    )(
        far(span_hidden),
        far(gain),
        far(key_value_weight),
        far(prompt_key_value),
        span_offset,
        cont_lengths,
        far(cont_query),
        far(continuation_key_value),
        far(rotary),
    )
    return pl.pallas_call(
        hand_on,
        out_shape=(
            jax.ShapeDtypeStruct((rows, width), BF16),
            jax.ShapeDtypeStruct((1, tokens, QUERY_HEADS * HEAD_SIZE), BF16),
        ),
        in_specs=[anywhere, anywhere],
        out_specs=(anywhere, anywhere),
        scratch_shapes=[dma((2,))],
        compiler_params=pltpu.CompilerParams(vmem_limit_bytes=1 << 20),
        name="hand_on",
    )(span_rows, attended)


def solution(mesh):
    placed = (
        P("parts", "seq"),
        P("seq"),
        P("seq", "set"),
        P(("parts", "seq"), None),
        P("parts"),
        P(("parts", "set", "seq"), None, None),
        P(("parts", "set", "seq"), None, None),
        P(("parts", "set", "seq")),
    )
    return jax.shard_map(
        functools.partial(on_device, mesh.shape["set"], mesh.shape["seq"]),
        mesh=mesh,
        in_specs=placed,
        out_specs=(P(("parts", "seq"), "set"), P(("parts", "set", "seq"), None, None)),
        check_vma=False,
    )
```
